128 devices in a mesh: pool: 16 (over x, z), rep: 8 (over y, core).
Axes of the slice: x: 4, y: 4, z: 4, core: 2. Of those that a mesh axis runs over, the one named last changes fastest.
Arguments:
- hidden: bfloat16 [8, 64, 2048], P('rep', 'pool'), may hold values from -6 to 6
- queries: bfloat16 [8, 64, 16, 192], P('rep', 'pool'), may hold values from -8 to 8
- new_kv: bfloat16 [8, 64, 576], P('rep', 'pool'), may hold values from -6 to 6
- kv_cache: bfloat16 [8, 768, 128, 576], P('rep', 'pool'), may hold values from -8 to 8
- block_table: int32 [8, 64, 128], P('rep'), may hold values from -1 to 767, as said below
- seq_lens: int32 [8, 64], P('rep'), may hold values from 1 to 16384, as said below
- w_uk: bfloat16 [16, 128, 512], replicated, may hold values from -0.5 to 0.5
- w_uv: bfloat16 [16, 512, 128], replicated, may hold values from -0.25 to 0.25
- o_proj: bfloat16 [2048, 2048], P('rep'), may hold values from -0.125 to 0.125
- norm_gain: float32 [2048], replicated, may hold values from 0.1 to 1.9
- routes: int32 [16, 8, 4, 6], P('pool'), may hold values from 0 to 63, all different within a row; in each aligned block of 32 rows (0 to 31, 32 to 63, ..., all dimensions but the last counted through in order) at most 6 rows name the same one
- gate_weights: float32 [16, 8, 4, 6], P('pool'), may hold values from 0.02 to 0.3
- w_gate: bfloat16 [64, 2048, 1408], P('pool', None, 'rep'), may hold values from -0.125 to 0.125
- w_up: bfloat16 [64, 2048, 1408], P('pool', None, 'rep'), may hold values from -0.125 to 0.125
- w_down: bfloat16 [64, 1408, 2048], P('pool', 'rep'), may hold values from -0.15625 to 0.15625
- shared_gate: bfloat16 [2048, 2816], P(None, 'rep'), may hold values from -0.125 to 0.125
- shared_up: bfloat16 [2048, 2816], P(None, 'rep'), may hold values from -0.125 to 0.125
- shared_down: bfloat16 [2816, 2048], P('rep'), may hold values from -0.109375 to 0.109375
Outputs:
- attn_out: bfloat16 [8, 64, 2048], P('rep', 'pool')
- layer_out: bfloat16 [8, 64, 2048], P('rep', 'pool')
The draws below stay inside these ranges and needn't reach their ends.
Inputs may be any that keep to these rules, and one draw needn't show every extreme that they name: `block_table`: entry (g, j, i) for i < ceil(seq_lens[g, j] / 128) names a page p of group g's 768 pages, page p lying on pool index p // 48; these pages are all different within a group; the other entries are -1. `seq_lens`: in every group one request has 16384 cached tokens. Each row names 6 different experts; among the 32 rows routes[p] of one pool index no expert is named more than 6 times.
All inputs are finite; a program needn't handle non-finite values.
Results may differ from the reference program's by a relative error of at most 0.02.
Values may be sent and summed in bfloat16 or wider, within the bound.
A program may use at most 128 MiB of HBM per device.

```python
import math
import jax
import jax.numpy as jnp
import numpy as np
from jax import lax

D = 2048
H = 16
NOPE = 128
ROPE = 64
LAT = 512
VD = 128
EXPERTS = 64
TOPK = 6
FF = 1408
SFF = 2816
RD = 4
PAGE = 128
MAXP = 128
KVW = 576
G = 8
REQ_GRP = 64
COLROWS = 32
PAGES_GRP = 768
USED = 672
CAP = 6
N_POOL = 16


def shuffle_pages(group_key):
    return jax.random.permutation(group_key, PAGES_GRP)


def pick_pages(row_perm, row_index):
    return row_perm[row_index]


def page_layout(key):
    base_key = jax.random.fold_in(key, 101)
    key_weight, key_big, key_fill, key_perm = jax.random.split(base_key, 4)
    draws = jax.random.randint(key_weight, (G, REQ_GRP), 1, 64)
    big_req = jax.random.randint(key_big, (G, 1), 0, REQ_GRP)
    others = jnp.arange(REQ_GRP)[None, :] != big_req
    spread = jnp.where(others, draws, 0)
    remainder = USED - MAXP - (REQ_GRP - 1)
    extra_pages = spread * remainder // jnp.sum(spread, axis=1, keepdims=True)
    counts = jnp.where(others, jnp.minimum(1 + extra_pages, MAXP), MAXP)
    last_fill = jax.random.randint(key_fill, (G, REQ_GRP), 1, PAGE + 1)
    lengths = jnp.where(others, (counts - 1) * PAGE + last_fill, MAXP * PAGE)
    permuted = jax.vmap(shuffle_pages)(jax.random.split(key_perm, G))
    starts = jnp.cumsum(counts, axis=1) - counts
    slot_ids = jnp.arange(MAXP)
    take_index = jnp.minimum(starts[:, :, None] + slot_ids[None, None, :], PAGES_GRP - 1)
    page_ids = jax.vmap(pick_pages)(permuted, take_index)
    page_table = jnp.where(slot_ids[None, None, :] < counts[:, :, None], page_ids, -1)
    return (page_table.astype(jnp.int32), lengths.astype(jnp.int32))


def draw_block_table(key, part):
    return page_layout(key)[0]


def draw_seq_lens(key, part):
    return page_layout(key)[1]


def draw_queries(key, part):
    key_main = jax.random.fold_in(jax.random.fold_in(key, 303), 0)
    full_shape = (G, REQ_GRP, H, NOPE + ROPE)
    values = jnp.clip(1.5 * jax.random.normal(key_main, full_shape, jnp.float32), -8.0, 8.0)
    return values.astype(jnp.bfloat16)


def draw_kv_cache(key, part):
    key_main = jax.random.fold_in(key, 404)
    full_shape = (G, PAGES_GRP, PAGE, LAT + ROPE)
    values = jnp.clip(jax.random.normal(key_main, full_shape, jnp.float32), -8.0, 8.0)
    return values.astype(jnp.bfloat16)


def level_of(rng, extent, pieces, low, top_value):
    def one(dim, blocks):
        steps = jax.random.uniform(jax.random.fold_in(jax.random.fold_in(rng, 6), dim), (blocks,), jnp.float32, low / len(pieces), top_value / len(pieces))
        return jnp.repeat(jnp.exp(steps), extent[dim] // blocks).reshape((-1,) + (1,) * (len(extent) - dim - 1))

    gain = one(*pieces[0])
    for cut in pieces[1:]:
        gain = gain * one(*cut)
    return gain


def deal_out(stream_key, own, number, rows, count, top, most, lean):
    sequence = jax.random.permutation(stream_key, count)
    crowded, ordinary = load_shares(count, rows * top, most, lean, True), load_shares(count, rows * top, most, lean, False)
    places = jnp.arange(count)

    def named(sizes, turn):
        used = int((sizes > 0).sum())
        fixed = max(1, used // 4)
        passed = fixed + (places - fixed + turn * (used - fixed)) % max(1, count - fixed)
        return jnp.zeros((count,), jnp.int32).at[sequence[jnp.where(places < fixed, places, passed)]].set(jnp.asarray(sizes, jnp.int32))

    sizes = jnp.where(number % 4 == 0, named(crowded, number // 4), named(ordinary, number - number // 4 - 1))
    mixed = jax.random.permutation(jax.random.fold_in(own, 3), count)
    donor, sink = mixed[0:count // 2 * 2:2], mixed[1:count // 2 * 2:2]
    room = jnp.minimum(sizes[donor] - 1, most - sizes[sink]) // 2
    room = jnp.where((donor == sequence[0]) | (sink == sequence[0]) | (sizes[sink] == 0), 0, jnp.maximum(room, 0))
    passed = jax.random.randint(jax.random.fold_in(own, 4), (count // 2,), 0, 1 << 20) % (room + 1)
    sizes = sizes.at[donor].add(-passed).at[sink].add(passed)
    items = jnp.searchsorted(jnp.cumsum(sizes), jnp.arange(rows * top), side="right").astype(jnp.int32)
    listing = items.reshape(top, rows).T
    listing = listing[jax.random.permutation(jax.random.fold_in(own, 1), rows)]
    turn = jax.random.randint(jax.random.fold_in(own, 2), (rows, 1), 0, top)
    return jnp.take_along_axis(listing, (jnp.arange(top)[None, :] + turn) % top, axis=1)


def load_shares(number_of, total, reach, lean, full):
    portions = [(1 << 20) // math.isqrt(grade ** lean) + 1 for grade in range(1, number_of + 1)]
    largest = reach if full else min(reach, max(-(-total // number_of), total * portions[0] // sum(portions)))
    least = 1 if total - largest >= number_of - 1 else 0
    holding, spare = [largest] + [least] * (number_of - 1), total - largest - least * (number_of - 1)
    while spare > 0:
        movable = [i for i in range(1, number_of) if holding[i] < largest] or [i for i in range(1, number_of) if holding[i] < reach]
        whole, left = sum([portions[i] for i in movable]), spare
        for i in movable:
            addition = min(reach - holding[i], max(1, left * portions[i] // whole), spare)
            holding[i] = holding[i] + addition
            spare = spare - addition
    return np.array(holding)


def bell_draw(stream_key, shape, width, bound, shards=(), kind=jnp.bfloat16):
    entries = jax.random.normal(stream_key, shape, jnp.float32) * width
    if len(shards) > 0:
        entries = level_of(stream_key, shape, shards, -0.22, 0.18) * entries
    return jnp.clip(entries, min=-bound, max=bound).astype(kind)


def setup_inputs(seed: int = 0) -> dict:
    key_of = jax.random.split(jax.random.key(seed), 19)
    hidden = bell_draw(key_of[0], (G, REQ_GRP, D), 1.0, 6.0, ((0, 8), (1, 16)))
    queries = draw_queries(jax.random.fold_in(key_of[18], 71), 0)
    new_kv = bell_draw(key_of[2], (G, REQ_GRP, KVW), 1.0, 6.0, ((0, 8), (1, 16)))
    kv_cache = draw_kv_cache(jax.random.fold_in(key_of[18], 71), 0)
    block_table = draw_block_table(jax.random.fold_in(key_of[18], 71), 0)
    seq_lens = draw_seq_lens(jax.random.fold_in(key_of[18], 71), 0)
    w_uk = bell_draw(key_of[6], (H, NOPE, LAT), NOPE ** -0.5, 0.5)
    w_uv = bell_draw(key_of[7], (H, LAT, VD), LAT ** -0.5, 0.25)
    o_proj = bell_draw(key_of[8], (H * VD, D), (H * VD) ** -0.5, 0.125, ((0, 8),))
    norm_gain = jnp.clip(1.0 + 0.18 * jax.random.normal(key_of[9], (D,), jnp.float32), 0.1, 1.9)
    routes_keys = jax.random.split(jax.random.fold_in(key_of[10], 1), N_POOL * G * RD // COLROWS)
    routes_turns = jax.random.permutation(jax.random.fold_in(key_of[10], 3), N_POOL * G * RD // COLROWS)
    routes = jax.vmap(lambda own, number: deal_out(jax.random.fold_in(key_of[10], 2), own, number, COLROWS, EXPERTS, TOPK, CAP, 2))(routes_keys, routes_turns).reshape((N_POOL, G, RD, TOPK))
    gate_weights = jnp.clip(0.02 + 0.28 * jax.random.uniform(key_of[11], (N_POOL, G, RD, TOPK), jnp.float32) ** level_of(key_of[11], (N_POOL, G, RD, TOPK), ((0, 16),), -0.2, 0.2), 0.02, 0.3)
    w_gate = bell_draw(key_of[12], (EXPERTS, D, FF), D ** -0.5, 0.125, ((0, 16), (2, 8)))
    w_up = bell_draw(key_of[13], (EXPERTS, D, FF), D ** -0.5, 0.125, ((0, 16), (2, 8)))
    w_down = bell_draw(key_of[14], (EXPERTS, FF, D), FF ** -0.5, 0.15625, ((0, 16), (1, 8)))
    shared_gate = bell_draw(key_of[15], (D, SFF), D ** -0.5, 0.125, ((1, 8),))
    shared_up = bell_draw(key_of[16], (D, SFF), D ** -0.5, 0.125, ((1, 8),))
    shared_down = bell_draw(key_of[17], (SFF, D), SFF ** -0.5, 0.109375, ((0, 8),))
    return dict(hidden=hidden, queries=queries, new_kv=new_kv, kv_cache=kv_cache, block_table=block_table, seq_lens=seq_lens, w_uk=w_uk, w_uv=w_uv, o_proj=o_proj, norm_gain=norm_gain, routes=routes, gate_weights=gate_weights, w_gate=w_gate, w_up=w_up, w_down=w_down, shared_gate=shared_gate, shared_up=shared_up, shared_down=shared_down)


very_negative = -1e+30
norm_eps = 1e-06
highest = lax.Precision.HIGHEST

def swiglu(rows_in, gate_w, up_w, down_w):
    gate_act = jnp.dot(rows_in, gate_w, preferred_element_type=jnp.float32)
    up_act = jnp.dot(rows_in, up_w, preferred_element_type=jnp.float32)
    inner_act = (jax.nn.silu(gate_act) * up_act).astype(jnp.bfloat16)
    return jnp.dot(inner_act, down_w, preferred_element_type=jnp.float32)

def reference(hidden, queries, new_kv, kv_cache, block_table, seq_lens, w_uk, w_uv, o_proj, norm_gain, routes, gate_weights, w_gate, w_up, w_down, shared_gate, shared_up, shared_down):
    scaling = (NOPE + ROPE) ** (-0.5)
    absorbed = jnp.einsum('gjhn,hnl->gjhl', queries[..., :NOPE].astype(jnp.float32), w_uk.astype(jnp.float32))
    fanned = (jnp.concatenate([absorbed, queries[..., NOPE:].astype(jnp.float32)], axis=-1) * scaling).astype(jnp.bfloat16)
    value_map = w_uv.astype(jnp.float32)

    def one_group(block_items):
        group_q, group_new, group_cache, group_table, group_len = block_items
        total_pages = group_cache.shape[0]
        counts = (group_len + PAGE - 1) // PAGE
        slot_ids = jnp.arange(MAXP, dtype=jnp.int32)
        is_live = slot_ids[None, :] < counts[:, None]
        target = jnp.where(is_live, group_table, total_pages).reshape(-1).astype(jnp.int32)
        request_ids = jnp.broadcast_to(jnp.arange(REQ_GRP, dtype=jnp.int32)[:, None], group_table.shape).reshape(-1)
        place_ids = jnp.broadcast_to(slot_ids[None, :], group_table.shape).reshape(-1)
        owner_req = jnp.zeros((total_pages,), jnp.int32).at[target].set(request_ids, mode='drop')
        place_of = jnp.zeros((total_pages,), jnp.int32).at[target].set(place_ids, mode='drop')
        is_used = jnp.zeros((total_pages,), jnp.int32).at[target].set(jnp.ones_like(request_ids), mode='drop') == 1
        tokens = place_of[:, None] * PAGE + jnp.arange(PAGE, dtype=jnp.int32)[None, :]
        is_valid = is_used[:, None] & (tokens < group_len[owner_req][:, None])
        cache_wide = group_cache.astype(jnp.float32)
        scores = jnp.einsum('ihc,itc->iht', group_q[owner_req].astype(jnp.float32), cache_wide)
        masked = jnp.where(is_valid[:, None, :], scores, very_negative)
        member = (owner_req[None, :] == jnp.arange(REQ_GRP, dtype=jnp.int32)[:, None]) & is_used[None, :]
        page_peak = lax.optimization_barrier(jnp.max(masked, axis=-1))
        cached_peak = lax.optimization_barrier(jnp.max(jnp.where(member[:, :, None], page_peak[None, :, :], very_negative), axis=1))
        own_score = jnp.einsum('jhc,jc->jh', group_q.astype(jnp.float32), group_new.astype(jnp.float32))
        peak_score = jnp.maximum(cached_peak, own_score)
        rounded = jnp.where(is_valid[:, None, :], jnp.exp(masked - peak_score[owner_req][:, :, None]), 0.0).astype(jnp.bfloat16)
        weights = lax.optimization_barrier(rounded).astype(jnp.float32)
        page_numer = jnp.einsum('iht,itl->ihl', weights, cache_wide[..., :LAT])
        member_f = member.astype(jnp.float32)
        numerator = jnp.einsum('ji,ihl->jhl', member_f, page_numer, precision=highest)
        denominator = jnp.einsum('ji,ih->jh', member_f, lax.optimization_barrier(jnp.sum(weights, axis=-1)), precision=highest)
        own_round = jnp.exp(own_score - peak_score).astype(jnp.bfloat16)
        own_weight = lax.optimization_barrier(own_round).astype(jnp.float32)
        numerator = numerator + own_weight[:, :, None] * group_new[:, None, :LAT].astype(jnp.float32)
        denominator = denominator + own_weight
        head_values = jnp.einsum('jhl,hlv->jhv', numerator, value_map, precision=highest) / denominator[:, :, None]
        return head_values.astype(jnp.bfloat16).reshape(REQ_GRP, H * VD)
    heads_all = lax.map(one_group, (fanned, new_kv, kv_cache, block_table, seq_lens))
    total_rows = G * REQ_GRP
    projected = jnp.dot(heads_all.reshape(total_rows, H * VD), o_proj, preferred_element_type=jnp.float32)
    residual = hidden.reshape(total_rows, D).astype(jnp.float32) + projected
    normed = (residual * lax.rsqrt(lax.optimization_barrier(jnp.mean(residual * residual, axis=-1, keepdims=True)) + norm_eps) * norm_gain).astype(jnp.bfloat16)
    choice_ids = jnp.transpose(routes, (1, 0, 2, 3)).reshape(total_rows, TOPK)
    choice_gates = jnp.transpose(gate_weights, (1, 0, 2, 3)).reshape(total_rows, TOPK)
    rows_most = min(N_POOL * CAP, total_rows)

    def expert_step(running, expert_id):
        is_hit = choice_ids == expert_id
        share_of = lax.optimization_barrier(jnp.sum(jnp.where(is_hit, choice_gates, 0.0), axis=1))
        order_key = jnp.where(jnp.any(is_hit, axis=1), 0, 1).astype(jnp.int32)
        picked = jnp.argsort(order_key, stable=True)[:rows_most].astype(jnp.int32)
        expert_out = swiglu(normed[picked], w_gate[expert_id], w_up[expert_id], w_down[expert_id])
        running = running.at[picked].add(expert_out * share_of[picked][:, None])
        return (running, None)
    routed, _ = lax.scan(expert_step, jnp.zeros((total_rows, D), jnp.float32), jnp.arange(EXPERTS, dtype=jnp.int32))
    shared_out = swiglu(normed, shared_gate, shared_up, shared_down)
    layer_out = (residual + routed + shared_out).astype(jnp.bfloat16).reshape(G, REQ_GRP, D)
    attn_out = projected.astype(jnp.bfloat16).reshape(G, REQ_GRP, D)
    return (attn_out, layer_out)
```

```python
import functools

import jax
import jax.numpy as jnp
from jax import lax
from jax.experimental import pallas as pl
from jax.experimental.pallas import tpu as pltpu
from jax.sharding import PartitionSpec as P

F32 = jnp.float32
BF16 = jnp.bfloat16
NEG = -1e30
EPS = 1e-06
NX = 4
MESH = pl.DeviceIdType.MESH
VM = pl.BlockSpec(memory_space=pltpu.VMEM)
HBM = pl.BlockSpec(memory_space=pl.ANY)
SM = pl.BlockSpec(memory_space=pltpu.SMEM)
NT = (((1,), (1,)), ((), ()))
LIMIT = 60 * 1024 * 1024


def dot(a, b):
    return jnp.dot(a, b, preferred_element_type=F32)


def dot_nt(a, b):
    return lax.dot_general(a, b, NT, preferred_element_type=F32)


def place():
    p = lax.axis_index("pool")
    r = lax.axis_index("rep")
    return p // NX, p % NX, r // 2, r % 2


def pool_peers(x, z):
    out = []
    for d in range(1, 16):
        dx, dz = d // 4, d % 4
        out.append((d, ((x + dx) % 4) * 4 + (z + dz) % 4))
    return out


def rep_peers(y, c):
    out = []
    for d in range(1, 8):
        dy, dc = d // 2, d % 2
        out.append((d, ((y + dy) % 4) * 2 + (c + dc) % 2))
    return out


def send(src, dst, ssem, rsem, pool=None, rep=None):
    dev = {}
    if pool is not None:
        dev["pool"] = pool
    if rep is not None:
        dev["rep"] = rep
    cp = pltpu.make_async_remote_copy(
        src_ref=src, dst_ref=dst, send_sem=ssem, recv_sem=rsem, device_id=dev, device_id_type=MESH
    )
    cp.start()
    return cp


def greet(pool_list, rep_list):
    bar = pltpu.get_barrier_semaphore()
    for _, q in pool_list:
        pl.semaphore_signal(bar, inc=1, device_id={"pool": q}, device_id_type=MESH)
    for _, q in rep_list:
        pl.semaphore_signal(bar, inc=1, device_id={"rep": q}, device_id_type=MESH)
    pl.semaphore_wait(bar, len(pool_list) + len(rep_list))


def gather_queries(q_ref, out_ref, ssem, rsem):
    x, z, y, c = place()
    me = x * 4 + z
    peers = pool_peers(x, z)
    greet(peers, [])
    cps = [send(q_ref, out_ref.at[me], ssem.at[d], rsem.at[d], pool=q) for d, q in peers]
    out_ref[me] = q_ref[...]
    for cp in cps:
        cp.wait()


def attention(
    meta, qg, wuk, wuv, cache, fresh, p_out, stat_out, kv, qf, fq, sb, lb, db, acc, of, sf, sem
):
    pages = 48
    chunk = 8
    scale = 192 ** (-0.5)
    loads = []
    for i in range(pages // chunk):
        s = pl.ds(i * chunk, chunk)
        cp = pltpu.make_async_copy(cache.at[s], kv.at[s], sem.at[i])
        cp.start()
        loads.append(cp)
    kv[pages] = fresh[...]

    @pl.loop(0, 64, unroll=4)
    def _(j):
        v = qg[j].astype(F32)
        s = pl.ds(pl.multiple_of(j * 16, 16), 16)
        qf[0, s, :] = v[:, 0:128]
        qf[1, s, 0:64] = v[:, 128:192]
        lb[s, :] = jnp.full((16, 128), NEG, F32)
        db[s, :] = jnp.zeros((16, 128), F32)
        for t in range(4):
            acc[t, s, :] = jnp.zeros((16, 128), F32)

    for h in range(16):
        s = pl.ds(h, 64, stride=16)
        qa = qf[0, s, :].astype(BF16)
        qb = qf[1, s, :]
        a = dot(qa, wuk[h]) * scale
        for t in range(4):
            fq[t, s, :] = a[:, t * 128 : (t + 1) * 128]
        fq[4, s, :] = qb * scale

    lane = lax.broadcasted_iota(jnp.int32, (16, 128), 1)

    def scores(i):
        j = meta[0, i]
        lo = meta[1, i]
        hi = meta[2, i]
        ik = jnp.minimum(i, pages)
        s = pl.ds(pl.multiple_of(j * 16, 16), 16)
        qa = jnp.concatenate([fq[t, s, :] for t in range(4)], axis=1).astype(BF16)
        qb = fq[4, s, :][:, 0:64].astype(BF16)
        v = dot(qa, kv[ik, 0:512, :]) + dot(qb, kv[ik, 512:576, :])
        v = jnp.where((lane >= lo) & (lane < hi), v, NEG)
        sb[i] = v
        m = jnp.broadcast_to(jnp.max(v, axis=1, keepdims=True), (16, 128))
        lb[s, :] = jnp.maximum(lb[s, :], m)

    def sums(i):
        j = meta[0, i]
        lo = meta[1, i]
        hi = meta[2, i]
        ik = jnp.minimum(i, pages)
        s = pl.ds(pl.multiple_of(j * 16, 16), 16)
        w = jnp.exp(sb[i] - lb[s, :])
        w = jnp.where((lane >= lo) & (lane < hi), w, 0.0).astype(BF16)
        den = jnp.sum(w.astype(F32), axis=1, keepdims=True)
        num = dot_nt(w, kv[ik, 0:512, :])
        db[s, :] = db[s, :] + jnp.broadcast_to(den, (16, 128))
        for t in range(4):
            acc[t, s, :] = acc[t, s, :] + num[:, t * 128 : (t + 1) * 128]

    for i in range(pages // chunk):
        loads[i].wait()

        @pl.loop(0, chunk // 4)
        def _(g, i=i):
            for u in range(4):
                scores(i * chunk + g * 4 + u)

    for u in range(4):
        scores(jnp.int32(pages + u))

    @pl.loop(0, (pages + 4) // 4)
    def _(g):
        for u in range(4):
            sums(g * 4 + u)

    lane64 = lax.broadcasted_iota(jnp.int32, (64, 128), 1)
    stat = jnp.zeros((64, 128), F32)
    for h in range(16):
        s = pl.ds(h, 64, stride=16)
        a = jnp.concatenate([acc[t, s, :] for t in range(4)], axis=1).astype(BF16)
        d = db[s, :]
        full = d > 0.0
        safe = jnp.where(full, d, 1.0)
        of[:, h * 128 : (h + 1) * 128] = dot(a, wuv[h]) / safe
        lse = jnp.where(full, lb[s, :] + jnp.log(safe), NEG)
        stat = jnp.where(lane64 == h, lse, stat)
    sf[...] = stat
    for d in range(16):
        p_out[d] = of[d * 4 : (d + 1) * 4, :].astype(BF16)
        stat_out[d] = sf[d * 4 : (d + 1) * 4, :]


WIDTHS = (384, 384, 256)
STARTS = (0, 384, 768)
ORDERS = (("x", "z", "y"), ("z", "y", "x"), ("y", "x", "z"))
AX = {"x": 0, "z": 1, "y": 2}


def rest(
    p_ref, st_ref, hid, gain, gates_in, oproj_h, wg_h, wu_h, wd_h, sg_h, su_h, sd_h,
    attn_out, layer_out,
    oproj, wg, wu, wd, sg, su, sd, wsem,
    rp, rst, gates, heads, hs, hb, hbf, pf, ps, pr, nown, npart, blk,
    x0, x1, x2, xm, inner, shin, y0, y1, y2, cs0, cs1, cs2, cr0, cr1, cr2,
    sb0, sb1, sb2, ra0, ra1, ra2, rb0, rb1, rb2, rc0, rc1, rc2,
    za0, za1, za2, zb0, zb1, zb2, fs, fr,
    psem, ssem, gsem, hsem, osem, nsem, asem, fsem, csem, rsem, lsem,
):
    x, z, y, c = place()
    me = x * 4 + z
    rp_me = y * 2 + c
    coord = {"x": x, "z": z, "y": y}
    pools = pool_peers(x, z)
    reps = rep_peers(y, c)
    mate = y * 2 + 1 - c
    xs = (x0, x1, x2)
    wl = []
    for i, (h, v) in enumerate(
        ((oproj_h, oproj), (sg_h, sg), (su_h, su), (sd_h, sd), (wg_h, wg), (wu_h, wu), (wd_h, wd))
    ):
        cp = pltpu.make_async_copy(h, v, wsem.at[i])
        cp.start()
        wl.append(cp)
    greet(pools, reps)

    sc = [send(st_ref.at[q], rst.at[me], ssem.at[0, d], ssem.at[1, d], pool=q) for d, q in pools]
    pc = [send(p_ref.at[q], rp.at[me], psem.at[0, d], psem.at[1, d], pool=q) for d, q in pools]
    gc = [send(gates_in, gates.at[me], gsem.at[0, d], gsem.at[1, d], pool=q) for d, q in pools]
    rst[me] = st_ref[me]
    rp[me] = p_ref[me]
    gates[me] = gates_in[...]
    for cp in sc:
        cp.wait()
    top = rst[0]
    for s in range(1, 16):
        top = jnp.maximum(top, rst[s])
    tot = jnp.zeros((4, 128), F32)
    for s in range(16):
        e = jnp.exp(rst[s] - top)
        rst[s] = e
        tot = tot + e
    inv = 1.0 / tot
    for cp in pc:
        cp.wait()

    heads[...] = jnp.zeros((4, 2048), F32)

    @pl.loop(0, 16)
    def _(s):
        w = rst[s] * inv
        for h in range(16):
            cols = slice(h * 128, (h + 1) * 128)
            heads[:, cols] = heads[:, cols] + w[:, h : h + 1] * rp[s, :, cols].astype(F32)

    for g in range(8):
        hs[g] = heads[:, g * 256 : (g + 1) * 256].astype(BF16)
    hc = [send(hs.at[q], hb.at[rp_me], hsem.at[0, d], hsem.at[1, d], rep=q) for d, q in reps]
    hb[rp_me] = hs[rp_me]
    wl[0].wait()
    for cp in hc:
        cp.wait()
    for g in range(8):
        hbf[g * 4 : (g + 1) * 4, :] = hb[g].astype(F32)
    pf[...] = dot(hbf[...].astype(BF16), oproj[...])
    for g in range(8):
        ps[g] = pf[g * 4 : (g + 1) * 4, :].astype(BF16)
    oc = [send(ps.at[q], pr.at[rp_me], osem.at[0, d], osem.at[1, d], rep=q) for d, q in reps]
    pr[rp_me] = ps[rp_me]
    for cp in oc:
        cp.wait()
    proj = pr[0].astype(F32)
    for g in range(1, 8):
        proj = proj + pr[g].astype(F32)
    attn_out[...] = proj.astype(BF16)
    res = hid[...].astype(F32) + proj
    ms = jnp.mean(res * res, axis=1, keepdims=True)
    normed = (res * lax.rsqrt(ms + EPS) * gain[...]).astype(BF16)

    nown[...] = normed
    cp = send(nown, npart, nsem.at[0], nsem.at[1], rep=mate)
    for g in gc:
        g.wait()
    cp.wait()
    mine = normed.astype(F32)
    theirs = npart[...].astype(F32)
    blk[0:4, :] = jnp.where(c == 0, mine, theirs)
    blk[4:8, :] = jnp.where(c == 0, theirs, mine)
    for t in range(3):
        for h in range(2):
            s = h * 1024 + STARTS[t]
            xs[t][h, x, z, y] = blk[:, s : s + WIDTHS[t]].astype(BF16)

    def region(t, stage, over=None):
        idx = [None, None, None]
        for s, a in enumerate(ORDERS[t]):
            if s < stage:
                idx[AX[a]] = pl.ds(0, 4)
            else:
                v = coord[a]
                if s == stage and over is not None:
                    v = (v + over) % 4
                idx[AX[a]] = pl.ds(v, 1)
        return tuple(idx)

    def peer(a, d):
        v = (coord[a] + d) % 4
        if a == "x":
            return {"pool": v * 4 + z}
        if a == "z":
            return {"pool": x * 4 + v}
        return {"rep": v * 2 + c}

    fwd = []
    moving = {}
    for stage in range(3):
        for t in range(3):
            if stage > 0:
                for d in range(1, 4):
                    moving[t, stage - 1, d].wait()
                    reg = (c,) + region(t, stage - 1, -d)
                    k = (stage - 1) * 3 + d - 1
                    fwd.append(
                        send(xs[t].at[reg], xs[t].at[reg], fsem.at[0, t, k], fsem.at[1, t, k], rep=mate)
                    )
            for d in range(1, 4):
                a = ORDERS[t][stage]
                reg = (c,) + region(t, stage)
                moving[t, stage, d] = send(
                    xs[t].at[reg], xs[t].at[reg],
                    asem.at[0, t, stage, d], asem.at[1, t, stage, d], **peer(a, d)
                )
    for t in range(3):
        for d in range(1, 4):
            moving[t, 2, d].wait()
            reg = (c,) + region(t, 2, -d)
            k = 6 + d - 1
            fwd.append(send(xs[t].at[reg], xs[t].at[reg], fsem.at[0, t, k], fsem.at[1, t, k], rep=mate))
    for cp in fwd:
        cp.wait()

    for t in range(3):
        for h in range(2):
            s = h * 1024 + STARTS[t]
            v = xs[t][h].astype(F32).reshape(512, WIDTHS[t]).astype(BF16)
            xm[:, s : s + WIDTHS[t]] = v

    for cp in wl[1:]:
        cp.wait()

    col = xm[pl.ds(pl.multiple_of(me * 32, 32), 32), :]
    ga = dot_nt(col, sg[...])
    ua = dot_nt(col, su[...])
    shin[...] = (ga / (1.0 + jnp.exp(-ga)) * ua).astype(BF16)

    gm = gates[...].reshape(512, 128)
    ids = lax.broadcasted_iota(jnp.int32, (128, 176), 0) % 64

    @pl.loop(0, 4)
    def _(e):
        ga = dot_nt(xm[...], wg[e])
        ua = dot_nt(xm[...], wu[e])
        gw = dot(gm, jnp.where(ids == me * 4 + e, 1.0, 0.0).astype(BF16))
        inner[e] = (ga / (1.0 + jnp.exp(-ga)) * ua * gw).astype(BF16)

    ys = (y0, y1, y2)
    css = (cs0, cs1, cs2)
    crs = (cr0, cr1, cr2)
    cc = []
    for mine_half in (False, True):
        half = c if mine_half else 1 - c
        for t in range(3):
            wdt = WIDTHS[t]
            cols = pl.ds(pl.multiple_of(half * 1024 + STARTS[t], 128), wdt)
            v = dot(inner[0], wd[0, :, cols])
            for e in range(1, 4):
                v = v + dot(inner[e], wd[e, :, cols])
            sh = dot(shin[...], sd[:, cols])
            ys[t][...] = v.reshape(4, 4, 4, 8, wdt)
            ys[t][x, z] = ys[t][x, z] + sh.reshape(4, 8, wdt)
            if not mine_half:
                css[t][...] = ys[t][...].astype(BF16)
                cc.append(send(css[t], crs[t], csem.at[0, t], csem.at[1, t], rep=mate))

    sbs = (sb0, sb1, sb2)
    ras, rbs, rcs = (ra0, ra1, ra2), (rb0, rb1, rb2), (rc0, rc1, rc2)
    zas, zbs = (za0, za1, za2), (zb0, zb1, zb2)

    def part(t, stage, at):
        idx = [None, None, None]
        for s, a in enumerate(ORDERS[t]):
            if s < stage:
                idx[AX[a]] = pl.ds(0, 4)
            elif s == stage:
                idx[AX[a]] = pl.ds(at, 1)
            else:
                idx[AX[a]] = pl.ds(0, 1)
        return tuple(idx)

    going = {}
    for t in range(3):
        cc[t].wait()
        tot = ys[t][...] + crs[t][...].astype(F32)
        ys[t][...] = tot
        sbs[t][...] = tot.astype(BF16)
        a = ORDERS[t][2]
        for d in range(1, 4):
            going[t, 2, d] = send(
                sbs[t].at[part(t, 2, (coord[a] + d) % 4)], ras[t].at[d],
                rsem.at[0, t, 2, d], rsem.at[1, t, 2, d], **peer(a, d)
            )
    for t in range(3):
        a = ORDERS[t][2]
        for d in range(1, 4):
            going[t, 2, d].wait()
        v = ys[t][part(t, 2, coord[a])]
        for d in range(1, 4):
            v = v + ras[t][d].astype(F32)
        ras[t][0] = v.astype(BF16)
        zas[t][...] = v
        a = ORDERS[t][1]
        for d in range(1, 4):
            going[t, 1, d] = send(
                ras[t].at[(0,) + part(t, 1, (coord[a] + d) % 4)], rbs[t].at[d],
                rsem.at[0, t, 1, d], rsem.at[1, t, 1, d], **peer(a, d)
            )
    for t in range(3):
        a = ORDERS[t][1]
        for d in range(1, 4):
            going[t, 1, d].wait()
        v = zas[t][part(t, 1, coord[a])]
        for d in range(1, 4):
            v = v + rbs[t][d].astype(F32)
        rbs[t][0] = v.astype(BF16)
        zbs[t][...] = v
        a = ORDERS[t][0]
        for d in range(1, 4):
            going[t, 0, d] = send(
                rbs[t].at[(0,) + part(t, 0, (coord[a] + d) % 4)], rcs[t].at[d],
                rsem.at[0, t, 0, d], rsem.at[1, t, 0, d], **peer(a, d)
            )
    for t in range(3):
        a = ORDERS[t][0]
        for d in range(1, 4):
            going[t, 0, d].wait()
        v = zbs[t][part(t, 0, coord[a])]
        for d in range(1, 4):
            v = v + rcs[t][d].astype(F32)
        blk[:, STARTS[t] : STARTS[t] + WIDTHS[t]] = v.reshape(8, WIDTHS[t])
    lo, hi = blk[0:4, 0:1024], blk[4:8, 0:1024]
    fs[...] = jnp.where(c == 0, hi, lo).astype(BF16)
    cp = send(fs, fr, lsem.at[0], lsem.at[1], rep=mate)
    own = jnp.where(c == 0, lo, hi)
    cp.wait()
    other = fr[...].astype(F32)
    layer_out[:, 0:1024] = (res[:, 0:1024] + jnp.where(c == 0, own, other)).astype(BF16)
    layer_out[:, 1024:2048] = (res[:, 1024:2048] + jnp.where(c == 0, other, own)).astype(BF16)


def dma(*shape):
    return pltpu.SemaphoreType.DMA(shape)


def rest_scratch():
    v = pltpu.VMEM
    out = [
        v((256, 2048), BF16), v((4, 176, 2048), BF16), v((4, 176, 2048), BF16), v((4, 176, 2048), BF16),
        v((352, 2048), BF16), v((352, 2048), BF16), v((352, 2048), BF16), dma(7),
        v((16, 4, 2048), BF16), v((16, 4, 128), F32), v((16, 32, 128), BF16), v((4, 2048), F32),
        v((8, 4, 256), BF16), v((8, 4, 256), BF16), v((32, 256), F32), v((32, 2048), F32),
        v((8, 4, 2048), BF16), v((8, 4, 2048), BF16), v((4, 2048), BF16), v((4, 2048), BF16),
        v((8, 2048), F32),
    ]
    out += [v((2, 4, 4, 4, 8, w), BF16) for w in WIDTHS]
    out += [v((512, 2048), BF16), v((4, 512, 176), BF16), v((32, 352), BF16)]
    out += [v((4, 4, 4, 8, w), F32) for w in WIDTHS]
    out += [v((4, 4, 4, 8, w), BF16) for w in WIDTHS] * 3

    def shape(t, stage):
        s = [1, 1, 1]
        for k, a in enumerate(ORDERS[t]):
            if k < stage:
                s[AX[a]] = 4
        return tuple(s) + (8, WIDTHS[t])

    for stage in (2, 1, 0):
        out += [v((4,) + shape(t, stage), BF16) for t in range(3)]
    for stage in (2, 1):
        out += [v(shape(t, stage), F32) for t in range(3)]
    out += [v((4, 1024), BF16), v((4, 1024), BF16)]
    out += [
        dma(2, 16), dma(2, 16), dma(2, 16), dma(2, 8), dma(2, 8), dma(2),
        dma(2, 3, 3, 4), dma(2, 3, 9), dma(2, 3), dma(2, 3, 3, 4), dma(2),
    ]
    return out


def params(cid=None):
    if cid is None:
        return pltpu.CompilerParams(vmem_limit_bytes=LIMIT)
    return pltpu.CompilerParams(vmem_limit_bytes=LIMIT, collective_id=cid, has_side_effects=True)


def shards(
    hidden,
    queries,
    new_kv,
    kv_cache,
    block_table,
    seq_lens,
    w_uk,
    w_uv,
    o_proj,
    norm_gain,
    routes,
    gate_weights,
    w_gate,
    w_up,
    w_down,
    shared_gate,
    shared_up,
    shared_down,
):
    pages = kv_cache.shape[1]
    pool_rank = lax.axis_index("pool")
    sds = jax.ShapeDtypeStruct

    table = block_table[0] - pool_rank * pages
    lengths = seq_lens[0]
    req = lax.broadcasted_iota(jnp.int32, table.shape, 0)
    slot = lax.broadcasted_iota(jnp.int32, table.shape, 1)
    filled = jnp.clip(lengths[:, None] - slot * 128, 0, 128)
    hit = (table[None] == jnp.arange(pages, dtype=jnp.int32)[:, None, None]) & (filled > 0)[None]
    code = jnp.sum(jnp.where(hit, (req * 256 + filled)[None], 0), axis=(1, 2))
    own = jnp.arange(4, dtype=jnp.int32)
    meta = jnp.stack(
        [
            jnp.concatenate([code // 256, pool_rank * 4 + own]),
            jnp.concatenate([jnp.zeros((pages,), jnp.int32), own]),
            jnp.concatenate([code % 256, own + 1]),
        ]
    )
    fresh = jnp.pad(new_kv[0].T, ((0, 0), (0, 124)))
    experts = jnp.arange(64, dtype=jnp.int32)
    dense = jnp.sum(
        jnp.where(routes[0].reshape(32, 6)[:, :, None] == experts, gate_weights[0].reshape(32, 6)[:, :, None], 0.0),
        axis=1,
    )
    coarse = dense.astype(BF16)
    gates = jnp.concatenate([coarse, (dense - coarse.astype(F32)).astype(BF16)], axis=1)

    qg = pl.pallas_call(
        gather_queries,
        out_shape=sds((16, 4, 16, 192), BF16),
        in_specs=[VM],
        out_specs=VM,
        scratch_shapes=[dma(16), dma(16)],
        compiler_params=params(0),
        name="gather_queries",
    )(queries[0])
    v = pltpu.VMEM
    parts, stats = pl.pallas_call(
        attention,
        out_shape=(sds((16, 4, 2048), BF16), sds((16, 4, 128), F32)),
        in_specs=[SM, VM, VM, VM, HBM, VM],
        out_specs=(VM, VM),
        scratch_shapes=[
            v((49, 576, 128), BF16), v((2, 1024, 128), F32), v((5, 1024, 128), F32), v((52, 16, 128), F32),
            v((1024, 128), F32), v((1024, 128), F32), v((4, 1024, 128), F32), v((64, 2048), F32),
            v((64, 128), F32), dma(6),
        ],
        compiler_params=params(),
        name="attention",
    )(meta, qg.reshape(64, 16, 192), w_uk, w_uv, jnp.swapaxes(kv_cache[0], 1, 2), fresh)
    wide = lambda w: jnp.swapaxes(w, -1, -2)
    attn, layer = pl.pallas_call(
        rest,
        out_shape=(sds((4, 2048), BF16), sds((4, 2048), BF16)),
        in_specs=[VM] * 5 + [HBM] * 7,
        out_specs=(VM, VM),
        scratch_shapes=rest_scratch(),
        compiler_params=params(1),
        name="rest",
    )(
        parts, stats, hidden[0], norm_gain[None], gates, o_proj, wide(w_gate), wide(w_up), w_down,
        wide(shared_gate), wide(shared_up), shared_down,
    )
    return attn[None], layer[None]


def solution(mesh):
    placed = (
        P("rep", "pool", None),
        P("rep", "pool", None, None),
        P("rep", "pool", None),
        P("rep", "pool", None, None),
        P("rep", None, None),
        P("rep", None),
        P(),
        P(),
        P("rep", None),
        P(),
        P("pool", None, None, None),
        P("pool", None, None, None),
        P("pool", None, "rep"),
        P("pool", None, "rep"),
        P("pool", "rep", None),
        P(None, "rep"),
        P(None, "rep"),
        P("rep", None),
    )
    return jax.shard_map(
        shards,
        mesh=mesh,
        in_specs=placed,
        out_specs=(P("rep", "pool", None), P("rep", "pool", None)),
        check_vma=False,
    )
```

```python
import functools

import jax
import jax.numpy as jnp
from jax import lax
from jax.experimental import pallas as pl
from jax.experimental.pallas import tpu as pltpu
from jax.sharding import PartitionSpec as P

F32 = jnp.float32
BF16 = jnp.bfloat16
NEG = -1e30
EPS = 1e-06
STOP = 99
NX = 4
MESH = pl.DeviceIdType.MESH
VM = pl.BlockSpec(memory_space=pltpu.VMEM)
HBM = pl.BlockSpec(memory_space=pl.ANY)
SM = pl.BlockSpec(memory_space=pltpu.SMEM)
NT = (((1,), (1,)), ((), ()))
LIMIT = 60 * 1024 * 1024


def dot(a, b):
    return jnp.dot(a, b, preferred_element_type=F32)


def dot_nt(a, b):
    return lax.dot_general(a, b, NT, preferred_element_type=F32)


def place():
    p = lax.axis_index("pool")
    r = lax.axis_index("rep")
    return p // NX, p % NX, r // 2, r % 2


def pool_peers(x, z):
    out = []
    for d in range(1, 16):
        dx, dz = d // 4, d % 4
        out.append((d, ((x + dx) % 4) * 4 + (z + dz) % 4))
    return out


def rep_peers(y, c):
    out = []
    for d in range(1, 8):
        dy, dc = d // 2, d % 2
        out.append((d, ((y + dy) % 4) * 2 + (c + dc) % 2))
    return out


def send(src, dst, ssem, rsem, pool=None, rep=None):
    dev = {}
    if pool is not None:
        dev["pool"] = pool
    if rep is not None:
        dev["rep"] = rep
    cp = pltpu.make_async_remote_copy(
        src_ref=src, dst_ref=dst, send_sem=ssem, recv_sem=rsem, device_id=dev, device_id_type=MESH
    )
    cp.start()
    return cp


def greet(devices):
    bar = pltpu.get_barrier_semaphore()
    for dev in devices:
        pl.semaphore_signal(bar, inc=1, device_id=dev, device_id_type=MESH)
    pl.semaphore_wait(bar, len(devices))


WIDTHS = (384, 384, 256)
STARTS = (0, 384, 768)
ORDERS = (("x", "z", "y"), ("z", "y", "x"), ("y", "x", "z"))
STEPS = (0, 1, 3, 2)
AX = {"x": 0, "z": 1, "y": 2}


def layer(
    q_in, table_in, len_in, new_in, hid, gain, gates_in,
    wuk_h, wuv_h, cache, oproj_h, wg_h, wu_h, wd_h, sg_h, su_h, sd_h,
    proj_out, moe_out,
    wuk, wuv, kv, oproj, wg, wu, wd, sg, su, sd, wsem, kvsem,
    qp, qg, qf, qr, fq, nb, mb, db, mrow, meta_v, wide, vb, of, sf, pbuf, stbuf, qsem,
    rp, rst, gates, heads, hs, hb, hbf, pf, ps, pr, nown, npart, blk,
    x0, x1, x2, xm, inner, shin, y0, y1, y2, cs0, cs1, cs2, cr0, cr1, cr2,
    sb0, sb1, sb2, ra0, ra1, ra2, rb0, rb1, rb2, fs, fr,
    psem, ssem, gsem, hsem, osem, nsem, asem, bsem, fsem, csem, dsem, esem, lsem,
):
    x, z, y, c = place()
    me = x * 4 + z
    rp_me = y * 2 + c
    coord = {"x": x, "z": z, "y": y}
    pools = pool_peers(x, z)
    reps = rep_peers(y, c)
    mate = y * 2 + 1 - c
    xs = (x0, x1, x2)
    pages, chunk, rows = 48, 8, 64
    scale = 192 ** (-0.5)

    def load(h, v, sem):
        cp = pltpu.make_async_copy(h, v, sem)
        cp.start()
        return cp

    wl = {0: load(wuk_h, wuk, wsem.at[0])}
    kl = []
    for i in range(pages // chunk):
        s = pl.ds(i * chunk, chunk)
        kl.append(load(cache.at[s], kv.at[s], kvsem.at[i]))
    def peer(**over):
        at = {a: (coord[a] + over.get(a, 0)) % 4 for a in "xzy"}
        return {"pool": at["x"] * 4 + at["z"], "rep": at["y"] * 2 + c}

    def more():
        for i, (h, v) in enumerate(
            ((wuv_h, wuv), (oproj_h, oproj), (sg_h, sg), (su_h, su), (sd_h, sd), (wg_h, wg), (wu_h, wu), (wd_h, wd))
        ):
            wl[i + 1] = load(h, v, wsem.at[i + 1])

    def bail(*waits):
        for cp in waits:
            cp.wait()
        proj_out[...] = jnp.zeros((4, 2048), F32)
        moe_out[...] = jnp.zeros((4, 2048), F32)

    for k in range(4):
        v = q_in[k].astype(F32)
        qp[k, 0:16, :] = v[:, 0:128].astype(BF16)
        qp[k, 16:24, :] = jnp.concatenate([v[0:8, 128:192], v[8:16, 128:192]], axis=1).astype(BF16)
    greet(
        [{"pool": q, "rep": rp_me} for _, q in pools]
        + [{"pool": me, "rep": q} for _, q in reps]
        + [peer(**{a: da, "y": dy}) for a in "xz" for da in range(1, 4) for dy in range(1, 4)]
    )
    if STOP == 0:
        return bail(*wl.values(), *kl)

    first = [send(qp, qg.at[x, z], qsem.at[0, d], qsem.at[1, d], pool=q) for d, q in pools]
    qg[x, z] = qp[...]

    sub = lax.broadcasted_iota(jnp.int32, (64, 128), 0)
    lane = lax.broadcasted_iota(jnp.int32, (64, 128), 1)
    lens = jnp.broadcast_to(len_in[...], (64, 64))
    diag = lax.broadcasted_iota(jnp.int32, (64, 64), 0) == lax.broadcasted_iota(jnp.int32, (64, 64), 1)
    lens = jnp.sum(jnp.where(diag, lens, 0), axis=1, keepdims=True)
    filled = jnp.clip(lens - lane * 128, 0, 128)
    code = sub * 256 + filled
    local = jnp.where(filled > 0, table_in[...] - me * pages, -1)
    for i in range(pages):
        mrow[i : i + 1, :] = jnp.sum(jnp.where(local == i, code, 0), axis=0, keepdims=True)
    mrow[pages:rows, :] = jnp.zeros((rows - pages, 128), jnp.int32)
    codes = jnp.broadcast_to(jnp.sum(mrow[...], axis=1, keepdims=True), (rows, 128))
    meta_v[...] = codes % 256
    virtual = (sub >= pages) & (sub < pages + 4)
    owner = jnp.where(virtual, me * 4 + sub - pages, codes // 256)

    wide[...] = jnp.zeros((128, 640), F32)
    wide[0:4, 0:576] = new_in[...].astype(F32)
    for t in range(5):
        n = 64 if t == 4 else 128
        kv[pages, t * 128 : t * 128 + n, :] = wide[:, t * 128 : (t + 1) * 128].T[0:n, :].astype(BF16)
    mb[pages * 16 + 64 :, :] = jnp.full(((rows - pages - 4) * 16, 128), NEG, F32)
    db[pages * 16 + 64 :, :] = jnp.zeros(((rows - pages - 4) * 16, 128), F32)
    for t in range(4):
        nb[t, pages * 16 + 64 :, :] = jnp.zeros(((rows - pages - 4) * 16, 128), F32)

    for cp in first:
        cp.wait()
    gc = [send(gates_in, gates.at[me], gsem.at[0, d], gsem.at[1, d], pool=q) for d, q in pools]
    gates[me] = gates_in[...]
    more()
    wl[0].wait()
    if STOP == 1:
        return bail(*[wl[i] for i in range(1, 9)], *kl, *gc)

    @pl.loop(0, 64, unroll=4)
    def _(j):
        v = qg[j // 16, (j // 4) % 4, j % 4].astype(F32)
        qf[pl.ds(pl.multiple_of(j * 16, 16), 16), :] = v[0:16]
        qr[pl.ds(pl.multiple_of(j * 8, 8), 8), :] = v[16:24]

    hot = jnp.where(lane == owner, 1.0, 0.0)
    pick = hot[:, 0:64].astype(BF16)
    for h in range(16):
        s = pl.ds(h, 64, stride=16)
        a = dot(dot(pick, qf[s, :].astype(BF16)).astype(BF16), wuk[h]) * scale
        for t in range(4):
            fq[t, s, :] = a[:, t * 128 : (t + 1) * 128]
        b = dot(pick, qr[pl.ds(h % 8, 64, stride=8), :].astype(BF16)) * scale
        if h >= 8:
            b = jnp.concatenate([b[:, 64:128], b[:, 0:64]], axis=1)
        fq[4, s, :] = b
    if STOP == 2:
        return bail(*[wl[i] for i in range(1, 9)], *kl, *gc)
    lane16 = lax.broadcasted_iota(jnp.int32, (16, 128), 1)

    def page(i, ik, lo, hi):
        s = pl.ds(pl.multiple_of(i * 16, 16), 16)
        qa = jnp.concatenate([fq[t, s, :] for t in range(4)], axis=1).astype(BF16)
        qb = fq[4, s, :][:, 0:64].astype(BF16)
        v = dot(qa, kv[ik, 0:512, :]) + dot(qb, kv[ik, 512:576, :])
        ok = (lane16 >= lo) & (lane16 < hi)
        v = jnp.where(ok, v, NEG)
        m = jnp.max(v, axis=1, keepdims=True)
        w = jnp.where(ok, jnp.exp(v - m), 0.0).astype(BF16)
        den = jnp.sum(w.astype(F32), axis=1, keepdims=True)
        num = dot_nt(w, kv[ik, 0:512, :])
        o = pl.ds(pl.multiple_of(i * 16, 16), 16)
        mb[o, :] = jnp.broadcast_to(m, (16, 128))
        db[o, :] = jnp.broadcast_to(den, (16, 128))
        for t in range(4):
            nb[t, o, :] = num[:, t * 128 : (t + 1) * 128]

    for k in range(4):
        page(pages + k, pages, k, k + 1)
    for cp in kl:
        cp.wait()

    @pl.loop(0, pages // 8)
    def _(g):
        for u in range(8):
            i = g * 8 + u
            page(i, i, 0, meta_v[pl.ds(i, 1), :])

    if STOP == 3:
        return bail(*[wl[i] for i in range(1, 9)], *gc)

    m = jnp.full((rows, 128), NEG, F32)
    d = jnp.zeros((rows, 128), F32)
    for h in range(16):
        s = pl.ds(h, rows, stride=16)
        m = jnp.where(lane == h, mb[s, :], m)
        d = jnp.where(lane == h, db[s, :], d)
    sf[...] = m
    meta_v[...] = owner
    lp = jnp.full((rows, 128), NEG, F32)
    lr = lp
    for i in range(pages + 4):
        o = meta_v[i : i + 1, :]
        row = sf[i : i + 1, :]
        lp = jnp.maximum(lp, jnp.where(owner == o, row, NEG))
        lr = jnp.maximum(lr, jnp.where(sub == o, row, NEG))
    e = jnp.exp(m - lp)
    hot = hot.T[0:64, :]
    rd = lax.dot_general(
        hot, e * d, (((1,), (0,)), ((), ())), preferred_element_type=F32, precision=lax.Precision.HIGHEST
    )
    wl[1].wait()
    for h in range(16):
        s = pl.ds(h, rows, stride=16)
        a = jnp.concatenate([nb[t, s, :] for t in range(4)], axis=1).astype(BF16)
        vb[:, h * 128 : (h + 1) * 128] = (dot(a, wuv[h]) * e[:, h : h + 1]).astype(BF16)
    full = rd > 0.0
    safe = jnp.where(full, rd, 1.0)
    inv = 1.0 / safe
    sf[...] = jnp.where(full, lr + jnp.log(safe), NEG)
    hot = hot.astype(BF16)
    for h in range(0, 16, 4):
        v = dot(hot, vb[:, h * 128 : (h + 4) * 128])
        for u in range(4):
            of[:, (h + u) * 128 : (h + u + 1) * 128] = v[:, u * 128 : (u + 1) * 128] * inv[:, h + u : h + u + 1]
    for k in range(16):
        pbuf[k] = of[k * 4 : (k + 1) * 4, :].astype(BF16)
        stbuf[k] = sf[k * 4 : (k + 1) * 4, :]
    if STOP == 4:
        return bail(*[wl[i] for i in range(2, 9)], *gc)
    sc = [send(stbuf.at[q], rst.at[me], ssem.at[0, d], ssem.at[1, d], pool=q) for d, q in pools]
    pc = [send(pbuf.at[q], rp.at[me], psem.at[0, d], psem.at[1, d], pool=q) for d, q in pools]
    rst[me] = stbuf[me]
    rp[me] = pbuf[me]
    for cp in sc:
        cp.wait()
    top = rst[0]
    for s in range(1, 16):
        top = jnp.maximum(top, rst[s])
    tot = jnp.zeros((4, 128), F32)
    for s in range(16):
        e = jnp.exp(rst[s] - top)
        rst[s] = e
        tot = tot + e
    inv = 1.0 / tot
    for cp in pc:
        cp.wait()

    heads[...] = jnp.zeros((4, 2048), F32)

    @pl.loop(0, 16)
    def _(s):
        w = rst[s] * inv
        for h in range(16):
            cols = slice(h * 128, (h + 1) * 128)
            heads[:, cols] = heads[:, cols] + w[:, h : h + 1] * rp[s, :, cols].astype(F32)

    if STOP == 5:
        return bail(*[wl[i] for i in range(2, 9)], *gc)
    for g in range(8):
        hs[g] = heads[:, g * 256 : (g + 1) * 256].astype(BF16)
    hc = [send(hs.at[q], hb.at[rp_me], hsem.at[0, d], hsem.at[1, d], rep=q) for d, q in reps]
    hb[rp_me] = hs[rp_me]
    wl[2].wait()
    for cp in hc:
        cp.wait()
    if STOP == 6:
        return bail(*[wl[i] for i in range(3, 9)], *gc)
    for g in range(8):
        hbf[g * 4 : (g + 1) * 4, :] = hb[g].astype(F32)
    pf[...] = dot(hbf[...].astype(BF16), oproj[...])
    for g in range(8):
        ps[g] = pf[g * 4 : (g + 1) * 4, :].astype(BF16)
    oc = [send(ps.at[q], pr.at[rp_me], osem.at[0, d], osem.at[1, d], rep=q) for d, q in reps]
    pr[rp_me] = ps[rp_me]
    for cp in oc:
        cp.wait()
    proj = pr[0].astype(F32)
    for g in range(1, 8):
        proj = proj + pr[g].astype(F32)
    proj_out[...] = proj
    res = hid[...].astype(F32) + proj
    ms = jnp.mean(res * res, axis=1, keepdims=True)
    normed = (res * lax.rsqrt(ms + EPS) * gain[...]).astype(BF16)

    if STOP == 7:
        return bail(*[wl[i] for i in range(3, 9)], *gc)
    nown[...] = normed
    cp = send(nown, npart, nsem.at[0], nsem.at[1], rep=mate)
    for g in gc:
        g.wait()
    cp.wait()
    mine = normed.astype(F32)
    theirs = npart[...].astype(F32)
    blk[0:4, :] = jnp.where(c == 0, mine, theirs)
    blk[4:8, :] = jnp.where(c == 0, theirs, mine)
    for t in range(3):
        s = pl.ds(pl.multiple_of(c * 1024 + STARTS[t], 128), WIDTHS[t])
        xs[t][c, x, z, y] = blk[:, s].astype(BF16)

    if STOP == 8:
        return bail(*[wl[i] for i in range(3, 9)])
    whole = pl.ds(0, 4)

    def idx(at):
        return tuple(at[a] if not isinstance(at[a], jax.Array) else pl.ds(at[a], 1) for a in "xzy")

    def near(a, d):
        return (coord[a] + d) % 4

    fwd = []

    def share(t, k, at):
        ref = xs[t].at[(c,) + idx(at)]
        fwd.append(send(ref, ref, fsem.at[0, t, k], fsem.at[1, t, k], rep=mate))

    flat = {}
    for da in STEPS:
        for db in STEPS:
            if da or db:
                for t in range(3):
                    a, b, _ = ORDERS[t]
                    ref = xs[t].at[(c,) + idx(coord)]
                    k = da * 4 + db
                    flat[t, k] = send(
                        ref, ref, asem.at[0, t, k], asem.at[1, t, k], **peer(**{a: da, b: db})
                    )
    last = {}
    for da in STEPS:
        for t in range(3):
            a, b, w = ORDERS[t]
            for db in range(4):
                if da or db:
                    flat[t, da * 4 + db].wait()
            at = {a: near(a, -da), b: whole, w: coord[w]}
            ref = xs[t].at[(c,) + idx(at)]
            for d in range(1, 4):
                k = da * 4 + d
                last[t, da, d] = send(ref, ref, bsem.at[0, t, k], bsem.at[1, t, k], **peer(**{w: d}))
    for t in range(3):
        a, b, w = ORDERS[t]
        share(t, 0, {a: whole, b: whole, w: coord[w]})
    for d in (1, 3, 2):
        for t in range(3):
            a, b, w = ORDERS[t]
            for da in STEPS:
                last[t, da, d].wait()
            share(t, d, {a: whole, b: whole, w: near(w, -d)})
    for cp in fwd:
        cp.wait()
    if STOP == 9:
        return bail(*[wl[i] for i in range(3, 9)])

    for t in range(3):
        for h in range(2):
            s = h * 1024 + STARTS[t]
            v = xs[t][h].astype(F32).reshape(512, WIDTHS[t]).astype(BF16)
            xm[:, s : s + WIDTHS[t]] = v

    for i in range(3, 9):
        wl[i].wait()

    col = xm[pl.ds(pl.multiple_of(me * 32, 32), 32), :]
    ga = dot_nt(col, sg[...])
    ua = dot_nt(col, su[...])
    shin[...] = (ga / (1.0 + jnp.exp(-ga)) * ua).astype(BF16)

    gm = gates[...].reshape(512, 128)
    ids = lax.broadcasted_iota(jnp.int32, (128, 176), 0) % 64

    @pl.loop(0, 4)
    def _(e):
        ga = dot_nt(xm[...], wg[e])
        ua = dot_nt(xm[...], wu[e])
        gw = dot(gm, jnp.where(ids == me * 4 + e, 1.0, 0.0).astype(BF16))
        inner[e] = (ga / (1.0 + jnp.exp(-ga)) * ua * gw).astype(BF16)

    if STOP == 10:
        return bail()
    ys = (y0, y1, y2)
    css = (cs0, cs1, cs2)
    crs = (cr0, cr1, cr2)
    cc = []

    def down(t, half):
        wdt = WIDTHS[t]
        cols = pl.ds(pl.multiple_of(half * 1024 + STARTS[t], 128), wdt)
        v = dot(inner[0], wd[0, :, cols])
        for e in range(1, 4):
            v = v + dot(inner[e], wd[e, :, cols])
        sh = dot(shin[...], sd[:, cols])
        ys[t][...] = v.reshape(4, 4, 4, 8, wdt)
        ys[t][x, z] = ys[t][x, z] + sh.reshape(4, 8, wdt)

    for t in range(3):
        down(t, 1 - c)
        css[t][...] = ys[t][...].astype(BF16)
        cc.append(send(css[t], crs[t], csem.at[0, t], csem.at[1, t], rep=mate))

    sbs = (sb0, sb1, sb2)
    ras, rbs = (ra0, ra1, ra2), (rb0, rb1, rb2)

    back = (2, 1, 3, 0)
    away = {}
    for t in range(3):
        down(t, c)
        cc[t].wait()
        tot = ys[t][...] + crs[t][...].astype(F32)
        ys[t][...] = tot
        sbs[t][...] = tot.astype(BF16)
        a, b, w = ORDERS[t]
        for da in back:
            for d in range(1, 4):
                src = sbs[t].at[idx({a: near(a, da), b: whole, w: near(w, d)})]
                dst = ras[t].at[(d,) + idx({a: near(a, da), b: whole, w: coord[w] * 0})]
                k = da * 4 + d
                away[t, da, d] = send(src, dst, dsem.at[0, t, k], dsem.at[1, t, k], **peer(**{w: d}))
    if STOP == 11:
        return bail(*away.values())
    home = {}
    own = {}
    for da in back:
        for t in range(3):
            a, b, w = ORDERS[t]
            for d in range(1, 4):
                away[t, da, d].wait()
            at = idx({a: near(a, da), b: whole, w: coord[w] * 0})
            v = ys[t][idx({a: near(a, da), b: whole, w: coord[w]})]
            for d in range(1, 4):
                v = v + ras[t][(d,) + at].astype(F32)
            ras[t][(0,) + at] = v.astype(BF16)
            for db in back:
                k = da * 4 + db
                if k:
                    ref = ras[t].at[(0,) + idx({a: near(a, da), b: near(b, db), w: coord[w] * 0})]
                    dst = rbs[t].at[(k,) + (pl.ds(0, 1),) * 3]
                    home[t, k] = send(ref, dst, esem.at[0, t, k], esem.at[1, t, k], **peer(**{a: da, b: db}))
    for t in range(3):
        a, b, w = ORDERS[t]
        v = ras[t][(0,) + idx({a: coord[a], b: coord[b], w: coord[w] * 0})].astype(F32)
        for k in range(1, 16):
            home[t, k].wait()
            v = v + rbs[t][k].astype(F32)
        blk[:, STARTS[t] : STARTS[t] + WIDTHS[t]] = v.reshape(8, WIDTHS[t])
    lo, hi = blk[0:4, 0:1024], blk[4:8, 0:1024]
    fs[...] = jnp.where(c == 0, hi, lo).astype(BF16)
    cp = send(fs, fr, lsem.at[0], lsem.at[1], rep=mate)
    own = jnp.where(c == 0, lo, hi)
    cp.wait()
    other = fr[...].astype(F32)
    moe_out[:, 0:1024] = jnp.where(c == 0, own, other)
    moe_out[:, 1024:2048] = jnp.where(c == 0, other, own)


def dma(*shape):
    return pltpu.SemaphoreType.DMA(shape)


def scratch():
    v = pltpu.VMEM
    i32 = jnp.int32
    big = [v((4, 176, 2048), BF16)] * 3 + [v((352, 2048), BF16)] * 3
    out = [v((16, 128, 512), BF16), v((16, 512, 128), BF16), v((49, 576, 128), BF16), v((256, 2048), BF16)]
    out += big + [dma(9), dma(6)]
    out += [
        v((4, 24, 128), BF16), v((4, 4, 4, 24, 128), BF16), v((1024, 128), F32), v((512, 128), F32),
        v((5, 1024, 128), F32), v((4, 1024, 128), F32), v((1024, 128), F32), v((1024, 128), F32),
        v((64, 128), i32), v((64, 128), i32), v((128, 640), F32),
        v((64, 2048), BF16), v((64, 2048), F32), v((64, 128), F32), v((16, 4, 2048), BF16),
        v((16, 4, 128), F32), dma(2, 16),
    ]
    out += [
        v((16, 4, 2048), BF16), v((16, 4, 128), F32), v((16, 32, 128), BF16), v((4, 2048), F32),
        v((8, 4, 256), BF16), v((8, 4, 256), BF16), v((32, 256), F32), v((32, 2048), F32),
        v((8, 4, 2048), BF16), v((8, 4, 2048), BF16), v((4, 2048), BF16), v((4, 2048), BF16),
        v((8, 2048), F32),
    ]
    out += [v((2, 4, 4, 4, 8, w), BF16) for w in WIDTHS]
    out += [v((512, 2048), BF16), v((4, 512, 176), BF16), v((32, 352), BF16)]
    out += [v((4, 4, 4, 8, w), F32) for w in WIDTHS]
    out += [v((4, 4, 4, 8, w), BF16) for w in WIDTHS] * 3

    def shape(t):
        return tuple(1 if a == ORDERS[t][2] else 4 for a in "xzy") + (8, WIDTHS[t])

    out += [v((4,) + shape(t), BF16) for t in range(3)]
    out += [v((16, 1, 1, 1, 8, w), BF16) for w in WIDTHS]
    out += [v((4, 1024), BF16), v((4, 1024), BF16)]
    out += [
        dma(2, 16), dma(2, 16), dma(2, 16), dma(2, 8), dma(2, 8), dma(2),
        dma(2, 3, 16), dma(2, 3, 16), dma(2, 3, 4), dma(2, 3), dma(2, 3, 16), dma(2, 3, 16), dma(2),
    ]
    return out


def params(cid):
    return pltpu.CompilerParams(vmem_limit_bytes=LIMIT, collective_id=cid, has_side_effects=True)


def call(q, table, lens, new, hid, gain, gates, *weights):
    sds = jax.ShapeDtypeStruct
    return pl.pallas_call(
        layer,
        out_shape=(sds((4, 2048), F32), sds((4, 2048), F32)),
        in_specs=[VM] * 7 + [HBM] * 10,
        out_specs=(VM, VM),
        scratch_shapes=scratch(),
        compiler_params=params(0),
        name="layer",
    )(q, table, lens, new, hid, gain, gates, *weights)


def shards(
    hidden,
    queries,
    new_kv,
    kv_cache,
    block_table,
    seq_lens,
    w_uk,
    w_uv,
    o_proj,
    norm_gain,
    routes,
    gate_weights,
    w_gate,
    w_up,
    w_down,
    shared_gate,
    shared_up,
    shared_down,
):
    experts = jnp.arange(64, dtype=jnp.int32)
    dense = jnp.sum(
        jnp.where(routes[0].reshape(32, 6)[:, :, None] == experts, gate_weights[0].reshape(32, 6)[:, :, None], 0.0),
        axis=1,
    )
    coarse = dense.astype(BF16)
    gates = jnp.concatenate([coarse, (dense - coarse.astype(F32)).astype(BF16)], axis=1)

    wide = lambda w: jnp.swapaxes(w, -1, -2)
    proj, moe = call(
        queries[0], block_table[0], seq_lens, new_kv[0], hidden[0], norm_gain[None], gates,
        w_uk, w_uv, wide(kv_cache[0]), o_proj, wide(w_gate), wide(w_up), w_down,
        wide(shared_gate), wide(shared_up), shared_down,
    )
    layer_out = (hidden[0].astype(F32) + proj + moe).astype(BF16)
    return proj.astype(BF16)[None], layer_out[None]


def solution(mesh):
    placed = (
        P("rep", "pool", None),
        P("rep", "pool", None, None),
        P("rep", "pool", None),
        P("rep", "pool", None, None),
        P("rep", None, None),
        P("rep", None),
        P(),
        P(),
        P("rep", None),
        P(),
        P("pool", None, None, None),
        P("pool", None, None, None),
        P("pool", None, "rep"),
        P("pool", None, "rep"),
        P("pool", "rep", None),
        P(None, "rep"),
        P(None, "rep"),
        P("rep", None),
    )
    return jax.shard_map(
        shards,
        mesh=mesh,
        in_specs=placed,
        out_specs=(P("rep", "pool", None), P("rep", "pool", None)),
        check_vma=False,
    )
```

```python
import functools

import jax
import jax.numpy as jnp
from jax import lax
from jax.experimental import pallas as pl
from jax.experimental.pallas import tpu as pltpu
from jax.sharding import PartitionSpec as P

F32 = jnp.float32
BF16 = jnp.bfloat16
NEG = -1e30
EPS = 1e-06
STOP = 99
NX = 4
MESH = pl.DeviceIdType.MESH
VM = pl.BlockSpec(memory_space=pltpu.VMEM)
HBM = pl.BlockSpec(memory_space=pl.ANY)
SM = pl.BlockSpec(memory_space=pltpu.SMEM)
NT = (((1,), (1,)), ((), ()))
LIMIT = 60 * 1024 * 1024


def dot(a, b):
    return jnp.dot(a, b, preferred_element_type=F32)


def dot_nt(a, b):
    return lax.dot_general(a, b, NT, preferred_element_type=F32)


def place():
    p = lax.axis_index("pool")
    r = lax.axis_index("rep")
    return p // NX, p % NX, r // 2, r % 2


def pool_peers(x, z):
    out = []
    for d in range(1, 16):
        dx, dz = d // 4, d % 4
        out.append((d, ((x + dx) % 4) * 4 + (z + dz) % 4))
    return out


def rep_peers(y, c):
    out = []
    for d in range(1, 8):
        dy, dc = d // 2, d % 2
        out.append((d, ((y + dy) % 4) * 2 + (c + dc) % 2))
    return out


def send(src, dst, ssem, rsem, pool=None, rep=None):
    dev = {}
    if pool is not None:
        dev["pool"] = pool
    if rep is not None:
        dev["rep"] = rep
    cp = pltpu.make_async_remote_copy(
        src_ref=src, dst_ref=dst, send_sem=ssem, recv_sem=rsem, device_id=dev, device_id_type=MESH
    )
    cp.start()
    return cp


def hail(devices):
    bar = pltpu.get_barrier_semaphore()
    for dev in devices:
        pl.semaphore_signal(bar, inc=1, device_id=dev, device_id_type=MESH)


def meet(devices):
    pl.semaphore_wait(pltpu.get_barrier_semaphore(), len(devices))


WIDTHS = (384, 384, 256)
STARTS = (0, 384, 768)
ORDERS = (("x", "z", "y"), ("z", "y", "x"), ("y", "x", "z"))
STEPS = (0, 1, 3, 2)
AX = {"x": 0, "z": 1, "y": 2}


def layer(
    q_in, table_in, len_in, new_in, hid, gain, routes_in, weights_in,
    wuk_h, wuv_h, cache, oproj_h, wg_h, wu_h, wd_h, sg_h, su_h, sd_h,
    proj_out, moe_out,
    wuk, wuv, kv, oproj, wg, wu, wd, sg, su, sd, wsem, kvsem,
    qp, qg, qf, qr, fq, nb, mb, db, mrow, meta_v, wide, vb, of, sf, pbuf, stbuf, qsem,
    rp, rst, gates_own, gates, heads, hs, hb, hbf, pf, ps, pr, nown, npart, blk,
    x0, x1, x2, xm, inner, shin, y0, y1, y2, cs0, cs1, cs2, cr0, cr1, cr2,
    sb0, sb1, sb2, ra0, ra1, ra2, rb0, rb1, rb2, fs, fr,
    psem, ssem, gsem, hsem, osem, nsem, asem, bsem, fsem, csem, dsem, esem, lsem,
):
    x, z, y, c = place()
    me = x * 4 + z
    rp_me = y * 2 + c
    coord = {"x": x, "z": z, "y": y}
    pools = pool_peers(x, z)
    reps = rep_peers(y, c)
    mate = y * 2 + 1 - c
    xs = (x0, x1, x2)
    pages, chunk, rows = 48, 8, 64
    scale = 192 ** (-0.5)

    def load(h, v, sem):
        cp = pltpu.make_async_copy(h, v, sem)
        cp.start()
        return cp

    wl = {0: load(wuk_h, wuk, wsem.at[0])}
    kl = []
    for i in range(pages // chunk):
        s = pl.ds(i * chunk, chunk)
        kl.append(load(cache.at[s], kv.at[s], kvsem.at[i]))
    def peer(**over):
        at = {a: (coord[a] + over.get(a, 0)) % 4 for a in "xzy"}
        return {"pool": at["x"] * 4 + at["z"], "rep": at["y"] * 2 + c}

    def more():
        for i, (h, v) in enumerate(
            ((wuv_h, wuv), (oproj_h, oproj), (sg_h, sg), (su_h, su), (sd_h, sd), (wg_h, wg), (wu_h, wu), (wd_h, wd))
        ):
            wl[i + 1] = load(h, v, wsem.at[i + 1])

    def bail(*waits):
        for cp in waits:
            cp.wait()
        proj_out[...] = jnp.zeros((4, 2048), F32)
        moe_out[...] = jnp.zeros((4, 2048), F32)

    known = (
        [{"pool": q, "rep": rp_me} for _, q in pools]
        + [{"pool": me, "rep": q} for _, q in reps]
        + [peer(**{a: da, "y": dy}) for a in "xz" for da in range(1, 4) for dy in range(1, 4)]
    )
    hail(known)
    for k in range(4):
        v = q_in[k].astype(F32)
        qp[k, 0:16, :] = v[:, 0:128].astype(BF16)
        qp[k, 16:24, :] = jnp.concatenate([v[0:8, 128:192], v[8:16, 128:192]], axis=1).astype(BF16)
    sub = lax.broadcasted_iota(jnp.int32, (64, 128), 0)
    lane = lax.broadcasted_iota(jnp.int32, (64, 128), 1)
    lens = jnp.broadcast_to(len_in[...], (64, 64))
    diag = lax.broadcasted_iota(jnp.int32, (64, 64), 0) == lax.broadcasted_iota(jnp.int32, (64, 64), 1)
    lens = jnp.sum(jnp.where(diag, lens, 0), axis=1, keepdims=True)
    filled = jnp.clip(lens - lane * 128, 0, 128)
    code = sub * 256 + filled
    local = jnp.where(filled > 0, table_in[...] - me * pages, -1)
    for i in range(pages):
        mrow[i : i + 1, :] = jnp.sum(jnp.where(local == i, code, 0), axis=0, keepdims=True)
    mrow[pages:rows, :] = jnp.zeros((rows - pages, 128), jnp.int32)
    codes = jnp.broadcast_to(jnp.sum(mrow[...], axis=1, keepdims=True), (rows, 128))
    meta_v[...] = codes % 256
    virtual = (sub >= pages) & (sub < pages + 4)
    owner = jnp.where(virtual, me * 4 + sub - pages, codes // 256)

    ids64 = lax.broadcasted_iota(jnp.int32, (64, 8), 0)
    row32 = lax.broadcasted_iota(jnp.int32, (32, 8), 0)
    col8 = lax.broadcasted_iota(jnp.int32, (32, 8), 1)
    coarse = jnp.zeros((32, 64), F32)
    fine = coarse
    for q in range(4):
        v = jnp.zeros((64, 8), F32)
        for k in range(6):
            v = v + jnp.where(routes_in[k, q : q + 1, :] == ids64, weights_in[k, q : q + 1, :], 0.0)
        high = v.astype(BF16)
        low = (v - high.astype(F32)).astype(BF16)
        at = jnp.where(row32 == col8 * 4 + q, 1.0, 0.0).astype(BF16)
        coarse = coarse + dot_nt(at, high)
        fine = fine + dot_nt(at, low)
    gates_own[...] = jnp.concatenate([coarse, fine], axis=1).astype(BF16)

    meet(known)
    if STOP == 0:
        return bail(*wl.values(), *kl)

    first = [send(qp, qg.at[x, z], qsem.at[0, d], qsem.at[1, d], pool=q) for d, q in pools]
    qg[x, z] = qp[...]
    if STOP == 20:
        return bail(*wl.values(), *kl, *first)

    wide[...] = jnp.zeros((128, 640), F32)
    wide[0:4, 0:576] = new_in[...].astype(F32)
    for t in range(5):
        n = 64 if t == 4 else 128
        kv[pages, t * 128 : t * 128 + n, :] = wide[:, t * 128 : (t + 1) * 128].T[0:n, :].astype(BF16)
    mb[pages * 16 + 64 :, :] = jnp.full(((rows - pages - 4) * 16, 128), NEG, F32)
    db[pages * 16 + 64 :, :] = jnp.zeros(((rows - pages - 4) * 16, 128), F32)
    for t in range(4):
        nb[t, pages * 16 + 64 :, :] = jnp.zeros(((rows - pages - 4) * 16, 128), F32)

    for cp in first:
        cp.wait()
    gc = [send(gates_own, gates.at[me], gsem.at[0, d], gsem.at[1, d], pool=q) for d, q in pools]
    gates[me] = gates_own[...]
    wl[0].wait()
    if STOP == 1:
        return bail(*kl, *gc)

    @pl.loop(0, 64, unroll=4)
    def _(j):
        v = qg[j // 16, (j // 4) % 4, j % 4].astype(F32)
        qf[pl.ds(pl.multiple_of(j * 16, 16), 16), :] = v[0:16]
        qr[pl.ds(pl.multiple_of(j * 8, 8), 8), :] = v[16:24]

    hot = jnp.where(lane == owner, 1.0, 0.0)
    pick = hot[:, 0:64].astype(BF16)
    for h in range(16):
        s = pl.ds(h, 64, stride=16)
        a = dot(dot(pick, qf[s, :].astype(BF16)).astype(BF16), wuk[h]) * scale
        for t in range(4):
            fq[t, s, :] = a[:, t * 128 : (t + 1) * 128]
        b = dot(pick, qr[pl.ds(h % 8, 64, stride=8), :].astype(BF16)) * scale
        if h >= 8:
            b = jnp.concatenate([b[:, 64:128], b[:, 0:64]], axis=1)
        fq[4, s, :] = b
    if STOP == 2:
        return bail(*kl, *gc)
    more()
    group = lax.broadcasted_iota(jnp.int32, (32, 256), 0) // 16
    spot = lax.broadcasted_iota(jnp.int32, (32, 256), 1) - group * 128

    def pair(i, one, two, lo, hi):
        s = pl.ds(pl.multiple_of(i * 16, 32), 32)
        qa = jnp.concatenate([fq[t, s, :] for t in range(4)], axis=1).astype(BF16)
        qb = fq[4, s, :][:, 0:64].astype(BF16)
        kk = jnp.concatenate([kv[one], kv[two]], axis=1)
        v = dot(qa, kk[0:512, :]) + dot(qb, kk[512:576, :])
        ok = (spot >= lo) & (spot < hi)
        v = jnp.where(ok, v, NEG)
        m = jnp.max(v, axis=1, keepdims=True)
        w = jnp.where(ok, jnp.exp(v - m), 0.0).astype(BF16)
        den = jnp.sum(w.astype(F32), axis=1, keepdims=True)
        num = dot_nt(w, kk[0:512, :])
        mb[s, :] = jnp.broadcast_to(m, (32, 128))
        db[s, :] = jnp.broadcast_to(den, (32, 128))
        for t in range(4):
            nb[t, s, :] = num[:, t * 128 : (t + 1) * 128]

    for k in (0, 2):
        pair(pages + k, pages, pages, group + k, group + k + 1)
    for cp in kl:
        cp.wait()

    @pl.loop(0, pages // 8)
    def _(g):
        for u in range(0, 8, 2):
            i = g * 8 + u
            hi = [jnp.broadcast_to(meta_v[pl.ds(i + n, 1), :], (16, 128)) for n in range(2)]
            hi = jnp.concatenate(hi, axis=0)
            pair(i, i, i + 1, 0, jnp.concatenate([hi, hi], axis=1))

    if STOP == 3:
        return bail(*[wl[i] for i in range(1, 9)], *gc)

    m = jnp.full((rows, 128), NEG, F32)
    d = jnp.zeros((rows, 128), F32)
    for h in range(16):
        s = pl.ds(h, rows, stride=16)
        m = jnp.where(lane == h, mb[s, :], m)
        d = jnp.where(lane == h, db[s, :], d)
    sf[...] = m
    meta_v[...] = owner
    lp = jnp.full((rows, 128), NEG, F32)
    lr = lp
    for i in range(pages + 4):
        o = meta_v[i : i + 1, :]
        row = sf[i : i + 1, :]
        lp = jnp.maximum(lp, jnp.where(owner == o, row, NEG))
        lr = jnp.maximum(lr, jnp.where(sub == o, row, NEG))
    e = jnp.exp(m - lp)
    hot = hot.T[0:64, :]
    rd = lax.dot_general(
        hot, e * d, (((1,), (0,)), ((), ())), preferred_element_type=F32, precision=lax.Precision.HIGHEST
    )
    wl[1].wait()
    for h in range(16):
        s = pl.ds(h, rows, stride=16)
        a = jnp.concatenate([nb[t, s, :] for t in range(4)], axis=1).astype(BF16)
        vb[:, h * 128 : (h + 1) * 128] = (dot(a, wuv[h]) * e[:, h : h + 1]).astype(BF16)
    full = rd > 0.0
    safe = jnp.where(full, rd, 1.0)
    inv = 1.0 / safe
    sf[...] = jnp.where(full, lr + jnp.log(safe), NEG)
    hot = hot.astype(BF16)
    for h in range(0, 16, 4):
        v = dot(hot, vb[:, h * 128 : (h + 4) * 128])
        for u in range(4):
            of[:, (h + u) * 128 : (h + u + 1) * 128] = v[:, u * 128 : (u + 1) * 128] * inv[:, h + u : h + u + 1]
    for k in range(16):
        pbuf[k] = of[k * 4 : (k + 1) * 4, :].astype(BF16)
        stbuf[k] = sf[k * 4 : (k + 1) * 4, :]
    if STOP == 4:
        return bail(*[wl[i] for i in range(2, 9)], *gc)
    sc = [send(stbuf.at[q], rst.at[me], ssem.at[0, d], ssem.at[1, d], pool=q) for d, q in pools]
    pc = [send(pbuf.at[q], rp.at[me], psem.at[0, d], psem.at[1, d], pool=q) for d, q in pools]
    rst[me] = stbuf[me]
    rp[me] = pbuf[me]
    for cp in sc:
        cp.wait()
    top = rst[0]
    for s in range(1, 16):
        top = jnp.maximum(top, rst[s])
    tot = jnp.zeros((4, 128), F32)
    for s in range(16):
        e = jnp.exp(rst[s] - top)
        rst[s] = e
        tot = tot + e
    inv = 1.0 / tot
    for cp in pc:
        cp.wait()

    heads[...] = jnp.zeros((4, 2048), F32)

    @pl.loop(0, 16)
    def _(s):
        w = rst[s] * inv
        for h in range(16):
            cols = slice(h * 128, (h + 1) * 128)
            heads[:, cols] = heads[:, cols] + w[:, h : h + 1] * rp[s, :, cols].astype(F32)

    if STOP == 5:
        return bail(*[wl[i] for i in range(2, 9)], *gc)
    for g in range(8):
        hs[g] = heads[:, g * 256 : (g + 1) * 256].astype(BF16)
    hc = [send(hs.at[q], hb.at[rp_me], hsem.at[0, d], hsem.at[1, d], rep=q) for d, q in reps]
    hb[rp_me] = hs[rp_me]
    wl[2].wait()
    for cp in hc:
        cp.wait()
    if STOP == 6:
        return bail(*[wl[i] for i in range(3, 9)], *gc)
    for g in range(8):
        hbf[g * 4 : (g + 1) * 4, :] = hb[g].astype(F32)
    pf[...] = dot(hbf[...].astype(BF16), oproj[...])
    for g in range(8):
        ps[g] = pf[g * 4 : (g + 1) * 4, :].astype(BF16)
    oc = [send(ps.at[q], pr.at[rp_me], osem.at[0, d], osem.at[1, d], rep=q) for d, q in reps]
    pr[rp_me] = ps[rp_me]
    for cp in oc:
        cp.wait()
    proj = pr[0].astype(F32)
    for g in range(1, 8):
        proj = proj + pr[g].astype(F32)
    proj_out[...] = proj
    res = hid[...].astype(F32) + proj
    ms = jnp.mean(res * res, axis=1, keepdims=True)
    normed = (res * lax.rsqrt(ms + EPS) * gain[...]).astype(BF16)

    if STOP == 7:
        return bail(*[wl[i] for i in range(3, 9)], *gc)
    nown[...] = normed
    cp = send(nown, npart, nsem.at[0], nsem.at[1], rep=mate)
    for g in gc:
        g.wait()
    cp.wait()
    mine = normed.astype(F32)
    theirs = npart[...].astype(F32)
    blk[0:4, :] = jnp.where(c == 0, mine, theirs)
    blk[4:8, :] = jnp.where(c == 0, theirs, mine)
    for t in range(3):
        s = pl.ds(pl.multiple_of(c * 1024 + STARTS[t], 128), WIDTHS[t])
        xs[t][c, x, z, y] = blk[:, s].astype(BF16)

    if STOP == 8:
        return bail(*[wl[i] for i in range(3, 9)])
    whole = pl.ds(0, 4)

    def idx(at):
        return tuple(at[a] if not isinstance(at[a], jax.Array) else pl.ds(at[a], 1) for a in "xzy")

    def near(a, d):
        return (coord[a] + d) % 4

    fwd = []

    def share(t, k, at):
        ref = xs[t].at[(c,) + idx(at)]
        fwd.append(send(ref, ref, fsem.at[0, t, k], fsem.at[1, t, k], rep=mate))

    flat = {}
    for da in STEPS:
        for db in STEPS:
            if da or db:
                for t in range(3):
                    a, b, _ = ORDERS[t]
                    ref = xs[t].at[(c,) + idx(coord)]
                    k = da * 4 + db
                    flat[t, k] = send(
                        ref, ref, asem.at[0, t, k], asem.at[1, t, k], **peer(**{a: da, b: db})
                    )
    last = {}
    for da in STEPS:
        for t in range(3):
            a, b, w = ORDERS[t]
            for db in range(4):
                if da or db:
                    flat[t, da * 4 + db].wait()
            at = {a: near(a, -da), b: whole, w: coord[w]}
            ref = xs[t].at[(c,) + idx(at)]
            for d in range(1, 4):
                k = da * 4 + d
                last[t, da, d] = send(ref, ref, bsem.at[0, t, k], bsem.at[1, t, k], **peer(**{w: d}))
    for t in range(3):
        a, b, w = ORDERS[t]
        share(t, 0, {a: whole, b: whole, w: coord[w]})
    for d in (1, 3, 2):
        for t in range(3):
            a, b, w = ORDERS[t]
            for da in STEPS:
                last[t, da, d].wait()
            share(t, d, {a: whole, b: whole, w: near(w, -d)})
    for cp in fwd:
        cp.wait()
    if STOP == 9:
        return bail(*[wl[i] for i in range(3, 9)])

    for t in range(3):
        for h in range(2):
            s = h * 1024 + STARTS[t]
            v = xs[t][h].astype(F32).reshape(512, WIDTHS[t]).astype(BF16)
            xm[:, s : s + WIDTHS[t]] = v

    for i in range(3, 9):
        wl[i].wait()

    col = xm[pl.ds(pl.multiple_of(me * 32, 32), 32), :]
    ga = dot_nt(col, sg[...])
    ua = dot_nt(col, su[...])
    shin[...] = (ga / (1.0 + jnp.exp(-ga)) * ua).astype(BF16)

    gm = gates[...].reshape(512, 128)
    for lo, hi in ((0, 256), (256, 512), (512, 704)):
        ga = dot_nt(xm[...], wg[lo:hi, :])
        ua = dot_nt(xm[...], wu[lo:hi, :])
        ids = lax.broadcasted_iota(jnp.int32, (128, hi - lo), 0) % 64
        unit = lax.broadcasted_iota(jnp.int32, (128, hi - lo), 1) + lo
        gw = dot(gm, jnp.where(ids == me * 4 + unit // 176, 1.0, 0.0).astype(BF16))
        inner[:, lo:hi] = (ga / (1.0 + jnp.exp(-ga)) * ua * gw).astype(BF16)

    if STOP == 10:
        return bail()
    ys = (y0, y1, y2)
    css = (cs0, cs1, cs2)
    crs = (cr0, cr1, cr2)
    cc = []

    def down(t, half):
        wdt = WIDTHS[t]
        cols = pl.ds(pl.multiple_of(half * 1024 + STARTS[t], 128), wdt)
        v = dot(inner[...], wd[:, cols])
        sh = dot(shin[...], sd[:, cols])
        ys[t][...] = v.reshape(4, 4, 4, 8, wdt)
        ys[t][x, z] = ys[t][x, z] + sh.reshape(4, 8, wdt)

    for t in range(3):
        down(t, 1 - c)
        css[t][...] = ys[t][...].astype(BF16)
        cc.append(send(css[t], crs[t], csem.at[0, t], csem.at[1, t], rep=mate))

    sbs = (sb0, sb1, sb2)
    ras, rbs = (ra0, ra1, ra2), (rb0, rb1, rb2)

    back = (2, 1, 3, 0)
    away = {}
    for t in range(3):
        down(t, c)
        cc[t].wait()
        tot = ys[t][...] + crs[t][...].astype(F32)
        ys[t][...] = tot
        sbs[t][...] = tot.astype(BF16)
        a, b, w = ORDERS[t]
        for da in back:
            for d in range(1, 4):
                src = sbs[t].at[idx({a: near(a, da), b: whole, w: near(w, d)})]
                dst = ras[t].at[(d,) + idx({a: near(a, da), b: whole, w: coord[w] * 0})]
                k = da * 4 + d
                away[t, da, d] = send(src, dst, dsem.at[0, t, k], dsem.at[1, t, k], **peer(**{w: d}))
    if STOP == 11:
        return bail(*away.values())
    home = {}
    own = {}
    for da in back:
        for t in range(3):
            a, b, w = ORDERS[t]
            for d in range(1, 4):
                away[t, da, d].wait()
            at = idx({a: near(a, da), b: whole, w: coord[w] * 0})
            v = ys[t][idx({a: near(a, da), b: whole, w: coord[w]})]
            for d in range(1, 4):
                v = v + ras[t][(d,) + at].astype(F32)
            ras[t][(0,) + at] = v.astype(BF16)
            for db in back:
                k = da * 4 + db
                if k:
                    ref = ras[t].at[(0,) + idx({a: near(a, da), b: near(b, db), w: coord[w] * 0})]
                    dst = rbs[t].at[(k,) + (pl.ds(0, 1),) * 3]
                    home[t, k] = send(ref, dst, esem.at[0, t, k], esem.at[1, t, k], **peer(**{a: da, b: db}))
    for t in range(3):
        a, b, w = ORDERS[t]
        v = ras[t][(0,) + idx({a: coord[a], b: coord[b], w: coord[w] * 0})].astype(F32)
        for k in range(1, 16):
            home[t, k].wait()
            v = v + rbs[t][k].astype(F32)
        blk[:, STARTS[t] : STARTS[t] + WIDTHS[t]] = v.reshape(8, WIDTHS[t])
    lo, hi = blk[0:4, 0:1024], blk[4:8, 0:1024]
    fs[...] = jnp.where(c == 0, hi, lo).astype(BF16)
    cp = send(fs, fr, lsem.at[0], lsem.at[1], rep=mate)
    own = jnp.where(c == 0, lo, hi)
    cp.wait()
    other = fr[...].astype(F32)
    moe_out[:, 0:1024] = jnp.where(c == 0, own, other)
    moe_out[:, 1024:2048] = jnp.where(c == 0, other, own)


def dma(*shape):
    return pltpu.SemaphoreType.DMA(shape)


def scratch():
    v = pltpu.VMEM
    i32 = jnp.int32
    big = [v((704, 2048), BF16)] * 3 + [v((352, 2048), BF16)] * 3
    out = [v((16, 128, 512), BF16), v((16, 512, 128), BF16), v((49, 576, 128), BF16), v((256, 2048), BF16)]
    out += big + [dma(9), dma(6)]
    out += [
        v((4, 24, 128), BF16), v((4, 4, 4, 24, 128), BF16), v((1024, 128), F32), v((512, 128), F32),
        v((5, 1024, 128), F32), v((4, 1024, 128), F32), v((1024, 128), F32), v((1024, 128), F32),
        v((64, 128), i32), v((64, 128), i32), v((128, 640), F32),
        v((64, 2048), BF16), v((64, 2048), F32), v((64, 128), F32), v((16, 4, 2048), BF16),
        v((16, 4, 128), F32), dma(2, 16),
    ]
    out += [
        v((16, 4, 2048), BF16), v((16, 4, 128), F32), v((32, 128), BF16), v((16, 32, 128), BF16), v((4, 2048), F32),
        v((8, 4, 256), BF16), v((8, 4, 256), BF16), v((32, 256), F32), v((32, 2048), F32),
        v((8, 4, 2048), BF16), v((8, 4, 2048), BF16), v((4, 2048), BF16), v((4, 2048), BF16),
        v((8, 2048), F32),
    ]
    out += [v((2, 4, 4, 4, 8, w), BF16) for w in WIDTHS]
    out += [v((512, 2048), BF16), v((512, 704), BF16), v((32, 352), BF16)]
    out += [v((4, 4, 4, 8, w), F32) for w in WIDTHS]
    out += [v((4, 4, 4, 8, w), BF16) for w in WIDTHS] * 3

    def shape(t):
        return tuple(1 if a == ORDERS[t][2] else 4 for a in "xzy") + (8, WIDTHS[t])

    out += [v((4,) + shape(t), BF16) for t in range(3)]
    out += [v((16, 1, 1, 1, 8, w), BF16) for w in WIDTHS]
    out += [v((4, 1024), BF16), v((4, 1024), BF16)]
    out += [
        dma(2, 16), dma(2, 16), dma(2, 16), dma(2, 8), dma(2, 8), dma(2),
        dma(2, 3, 16), dma(2, 3, 16), dma(2, 3, 4), dma(2, 3), dma(2, 3, 16), dma(2, 3, 16), dma(2),
    ]
    return out


def params(cid):
    return pltpu.CompilerParams(vmem_limit_bytes=LIMIT, collective_id=cid, has_side_effects=True)


def call(q, table, lens, new, hid, gain, routes, gates, *weights):
    sds = jax.ShapeDtypeStruct
    return pl.pallas_call(
        layer,
        out_shape=(sds((4, 2048), F32), sds((4, 2048), F32)),
        in_specs=[VM] * 8 + [HBM] * 10,
        out_specs=(VM, VM),
        scratch_shapes=scratch(),
        compiler_params=params(0),
        name="layer",
    )(q, table, lens, new, hid, gain, routes, gates, *weights)


def shards(
    hidden,
    queries,
    new_kv,
    kv_cache,
    block_table,
    seq_lens,
    w_uk,
    w_uv,
    o_proj,
    norm_gain,
    routes,
    gate_weights,
    w_gate,
    w_up,
    w_down,
    shared_gate,
    shared_up,
    shared_down,
):
    wide = lambda w: jnp.swapaxes(w, -1, -2)
    flat = lambda w: w.reshape(-1, w.shape[-1])
    proj, moe = call(
        queries[0], block_table[0], seq_lens, new_kv[0], hidden[0], norm_gain[None],
        routes[0].T, gate_weights[0].T,
        w_uk, w_uv, wide(kv_cache[0]), o_proj, flat(wide(w_gate)), flat(wide(w_up)), flat(w_down),
        wide(shared_gate), wide(shared_up), shared_down,
    )
    layer_out = (hidden[0].astype(F32) + proj + moe).astype(BF16)
    return proj.astype(BF16)[None], layer_out[None]


def solution(mesh):
    placed = (
        P("rep", "pool", None),
        P("rep", "pool", None, None),
        P("rep", "pool", None),
        P("rep", "pool", None, None),
        P("rep", None, None),
        P("rep", None),
        P(),
        P(),
        P("rep", None),
        P(),
        P("pool", None, None, None),
        P("pool", None, None, None),
        P("pool", None, "rep"),
        P("pool", None, "rep"),
        P("pool", "rep", None),
        P(None, "rep"),
        P(None, "rep"),
        P("rep", None),
    )
    return jax.shard_map(
        shards,
        mesh=mesh,
        in_specs=placed,
        out_specs=(P("rep", "pool", None), P("rep", "pool", None)),
        check_vma=False,
    )
```

```python
import functools

import jax
import jax.numpy as jnp
from jax import lax
from jax.experimental import pallas as pl
from jax.experimental.pallas import tpu as pltpu
from jax.sharding import PartitionSpec as P

F32 = jnp.float32
BF16 = jnp.bfloat16
NEG = -1e30
EPS = 1e-06
NX = 4
MESH = pl.DeviceIdType.MESH
VM = pl.BlockSpec(memory_space=pltpu.VMEM)
HBM = pl.BlockSpec(memory_space=pl.ANY)
SM = pl.BlockSpec(memory_space=pltpu.SMEM)
NT = (((1,), (1,)), ((), ()))
LIMIT = 60 * 1024 * 1024


def dot(a, b):
    return jnp.dot(a, b, preferred_element_type=F32)


def dot_nt(a, b):
    return lax.dot_general(a, b, NT, preferred_element_type=F32)


def place():
    p = lax.axis_index("pool")
    r = lax.axis_index("rep")
    return p // NX, p % NX, r // 2, r % 2


def pool_peers(x, z):
    out = []
    for d in range(1, 16):
        dx, dz = d // 4, d % 4
        out.append((d, ((x + dx) % 4) * 4 + (z + dz) % 4))
    return out


def rep_peers(y, c):
    out = []
    for d in range(1, 8):
        dy, dc = d // 2, d % 2
        out.append((d, ((y + dy) % 4) * 2 + (c + dc) % 2))
    return out


def send(src, dst, ssem, rsem, pool=None, rep=None):
    dev = {}
    if pool is not None:
        dev["pool"] = pool
    if rep is not None:
        dev["rep"] = rep
    cp = pltpu.make_async_remote_copy(
        src_ref=src, dst_ref=dst, send_sem=ssem, recv_sem=rsem, device_id=dev, device_id_type=MESH
    )
    cp.start()
    return cp


def settle(ref, *sems):
    for sem in sems:
        pltpu.make_async_copy(ref, ref, sem).wait()


def hail(devices):
    bar = pltpu.get_barrier_semaphore()
    for dev in devices:
        pl.semaphore_signal(bar, inc=1, device_id=dev, device_id_type=MESH)


def meet(devices):
    pl.semaphore_wait(pltpu.get_barrier_semaphore(), len(devices))


WIDTHS = (384, 384, 256)
STARTS = (0, 384, 768)
ORDERS = (("x", "z", "y"), ("z", "y", "x"), ("y", "x", "z"))
STEPS = (0, 1, 3, 2)
AX = {"x": 0, "z": 1, "y": 2}


def layer(
    q_in, table_in, len_in, new_in, hid, gain, routes_in, weights_in,
    wuk_h, wuv_h, cache, oproj_h, wg_h, wu_h, wd_h, sg_h, su_h, sd_h,
    proj_out, moe_out,
    wuk, wuv, kv, oproj, wg, wu, wd, sg, su, sd, wsem, kvsem,
    qp, qg, qf, qr, fq, nb, mb, db, mrow, meta_v, wide, vb, of, sf, pbuf, stbuf, qsem,
    rp, rst, gates_own, gates, heads, hs, hb, hbf, pf, ps, pr, nown, npart, blk,
    x0, x1, x2, xm, inner, shin, y0, y1, y2, cs0, cs1, cs2, cr0, cr1, cr2,
    sb0, sb1, sb2, ra0, ra1, ra2, rb0, rb1, rb2, fs, fr,
    psem, ssem, gsem, hsem, osem, nsem, asem, bsem, fsem, csem, dsem, esem, lsem,
):
    x, z, y, c = place()
    me = x * 4 + z
    rp_me = y * 2 + c
    coord = {"x": x, "z": z, "y": y}
    pools = pool_peers(x, z)
    reps = rep_peers(y, c)
    mate = y * 2 + 1 - c
    xs = (x0, x1, x2)
    ras, rbs = (ra0, ra1, ra2), (rb0, rb1, rb2)
    pages, rows = 48, 64
    scale = 192 ** (-0.5)

    def load(h, v, sem):
        cp = pltpu.make_async_copy(h, v, sem)
        cp.start()
        return cp

    wl = {0: load(wuk_h, wuk, wsem.at[0])}
    kl = load(cache, kv.at[pl.ds(0, pages)], kvsem)

    def peer(**over):
        at = {a: (coord[a] + over.get(a, 0)) % 4 for a in "xzy"}
        return {"pool": at["x"] * 4 + at["z"], "rep": at["y"] * 2 + c}

    def more():
        for i, (h, v) in enumerate(
            ((wuv_h, wuv), (oproj_h, oproj), (sg_h, sg), (su_h, su), (sd_h, sd), (wg_h, wg), (wu_h, wu), (wd_h, wd))
        ):
            wl[i + 1] = load(h, v, wsem.at[i + 1])

    known = (
        [{"pool": q, "rep": rp_me} for _, q in pools]
        + [{"pool": me, "rep": q} for _, q in reps]
        + [peer(**{a: da, "y": dy}) for a in "xz" for da in range(1, 4) for dy in range(1, 4)]
    )
    hail(known)
    for k in range(4):
        v = q_in[k].astype(F32)
        qp[k, 0:16, :] = v[:, 0:128].astype(BF16)
        qp[k, 16:24, :] = jnp.concatenate([v[0:8, 128:192], v[8:16, 128:192]], axis=1).astype(BF16)
    sub = lax.broadcasted_iota(jnp.int32, (64, 128), 0)
    lane = lax.broadcasted_iota(jnp.int32, (64, 128), 1)
    lens = jnp.broadcast_to(len_in[...], (64, 64))
    diag = lax.broadcasted_iota(jnp.int32, (64, 64), 0) == lax.broadcasted_iota(jnp.int32, (64, 64), 1)
    lens = jnp.sum(jnp.where(diag, lens, 0), axis=1, keepdims=True)
    filled = jnp.clip(lens - lane * 128, 0, 128)
    code = sub * 256 + filled
    local = jnp.where(filled > 0, table_in[...] - me * pages, -1)
    for i in range(pages):
        mrow[i : i + 1, :] = jnp.sum(jnp.where(local == i, code, 0), axis=0, keepdims=True)
    mrow[pages:rows, :] = jnp.zeros((rows - pages, 128), jnp.int32)
    codes = jnp.broadcast_to(jnp.sum(mrow[...], axis=1, keepdims=True), (rows, 128))
    meta_v[...] = codes % 256
    virtual = (sub >= pages) & (sub < pages + 4)
    owner = jnp.where(virtual, me * 4 + sub - pages, codes // 256)

    ids64 = lax.broadcasted_iota(jnp.int32, (64, 8), 0)
    row32 = lax.broadcasted_iota(jnp.int32, (32, 8), 0)
    col8 = lax.broadcasted_iota(jnp.int32, (32, 8), 1)
    coarse = jnp.zeros((32, 64), F32)
    fine = coarse
    for q in range(4):
        v = jnp.zeros((64, 8), F32)
        for k in range(6):
            v = v + jnp.where(routes_in[k, q : q + 1, :] == ids64, weights_in[k, q : q + 1, :], 0.0)
        high = v.astype(BF16)
        low = (v - high.astype(F32)).astype(BF16)
        at = jnp.where(row32 == col8 * 4 + q, 1.0, 0.0).astype(BF16)
        coarse = coarse + dot_nt(at, high)
        fine = fine + dot_nt(at, low)
    gates_own[...] = jnp.concatenate([coarse, fine], axis=1).astype(BF16)

    meet(known)

    for _, q in pools:
        send(qp, qg.at[me], qsem.at[0], qsem.at[1], pool=q)
    qg[me] = qp[...]

    wide[...] = jnp.zeros((128, 640), F32)
    wide[0:4, 0:576] = new_in[...].astype(F32)
    for t in range(5):
        n = 64 if t == 4 else 128
        kv[pages, t * 128 : t * 128 + n, :] = wide[:, t * 128 : (t + 1) * 128].T[0:n, :].astype(BF16)
    mb[pages * 16 + 64 :, :] = jnp.full(((rows - pages - 4) * 16, 128), NEG, F32)
    db[pages * 16 + 64 :, :] = jnp.zeros(((rows - pages - 4) * 16, 128), F32)
    for t in range(4):
        nb[t, pages * 16 + 64 :, :] = jnp.zeros(((rows - pages - 4) * 16, 128), F32)

    settle(qg.at[pl.ds(0, 15)], qsem.at[0], qsem.at[1])
    for _, q in pools:
        send(gates_own, gates.at[me], gsem.at[0], gsem.at[1], pool=q)
    gates[me] = gates_own[...]
    wl[0].wait()

    @pl.loop(0, 64, unroll=4)
    def _(j):
        v = qg[j // 4, j % 4].astype(F32)
        qf[pl.ds(pl.multiple_of(j * 16, 16), 16), :] = v[0:16]
        qr[pl.ds(pl.multiple_of(j * 8, 8), 8), :] = v[16:24]

    hot = jnp.where(lane == owner, 1.0, 0.0)
    pick = hot[:, 0:64].astype(BF16)
    for h in range(16):
        s = pl.ds(h, 64, stride=16)
        a = dot(dot(pick, qf[s, :].astype(BF16)).astype(BF16), wuk[h]) * scale
        for t in range(4):
            fq[t, s, :] = a[:, t * 128 : (t + 1) * 128]
        b = dot(pick, qr[pl.ds(h % 8, 64, stride=8), :].astype(BF16)) * scale
        if h >= 8:
            b = jnp.concatenate([b[:, 64:128], b[:, 0:64]], axis=1)
        fq[4, s, :] = b
    more()
    group = lax.broadcasted_iota(jnp.int32, (32, 256), 0) // 16
    spot = lax.broadcasted_iota(jnp.int32, (32, 256), 1) - group * 128

    def pair(i, one, two, lo, hi):
        s = pl.ds(pl.multiple_of(i * 16, 32), 32)
        qa = jnp.concatenate([fq[t, s, :] for t in range(4)], axis=1).astype(BF16)
        qb = fq[4, s, :][:, 0:64].astype(BF16)
        kk = jnp.concatenate([kv[one], kv[two]], axis=1)
        v = dot(qa, kk[0:512, :]) + dot(qb, kk[512:576, :])
        ok = (spot >= lo) & (spot < hi)
        v = jnp.where(ok, v, NEG)
        m = jnp.max(v, axis=1, keepdims=True)
        w = jnp.where(ok, jnp.exp(v - m), 0.0).astype(BF16)
        den = jnp.sum(w.astype(F32), axis=1, keepdims=True)
        num = dot_nt(w, kk[0:512, :])
        mb[s, :] = jnp.broadcast_to(m, (32, 128))
        db[s, :] = jnp.broadcast_to(den, (32, 128))
        for t in range(4):
            nb[t, s, :] = num[:, t * 128 : (t + 1) * 128]

    for k in (0, 2):
        pair(pages + k, pages, pages, group + k, group + k + 1)
    kl.wait()

    @pl.loop(0, pages // 8)
    def _(g):
        for u in range(0, 8, 2):
            i = g * 8 + u
            hi = [jnp.broadcast_to(meta_v[pl.ds(i + n, 1), :], (16, 128)) for n in range(2)]
            hi = jnp.concatenate(hi, axis=0)
            pair(i, i, i + 1, 0, jnp.concatenate([hi, hi], axis=1))


    m = jnp.full((rows, 128), NEG, F32)
    d = jnp.zeros((rows, 128), F32)
    for h in range(16):
        s = pl.ds(h, rows, stride=16)
        m = jnp.where(lane == h, mb[s, :], m)
        d = jnp.where(lane == h, db[s, :], d)
    sf[...] = m
    meta_v[...] = owner
    lp = jnp.full((rows, 128), NEG, F32)
    lr = lp
    for i in range(pages + 4):
        o = meta_v[i : i + 1, :]
        row = sf[i : i + 1, :]
        lp = jnp.maximum(lp, jnp.where(owner == o, row, NEG))
        lr = jnp.maximum(lr, jnp.where(sub == o, row, NEG))
    e = jnp.exp(m - lp)
    hot = hot.T[0:64, :]
    rd = lax.dot_general(
        hot, e * d, (((1,), (0,)), ((), ())), preferred_element_type=F32, precision=lax.Precision.HIGHEST
    )
    wl[1].wait()
    for h in range(16):
        s = pl.ds(h, rows, stride=16)
        a = jnp.concatenate([nb[t, s, :] for t in range(4)], axis=1).astype(BF16)
        vb[:, h * 128 : (h + 1) * 128] = (dot(a, wuv[h]) * e[:, h : h + 1]).astype(BF16)
    full = rd > 0.0
    safe = jnp.where(full, rd, 1.0)
    inv = 1.0 / safe
    sf[...] = jnp.where(full, lr + jnp.log(safe), NEG)
    hot = hot.astype(BF16)
    for h in range(0, 16, 4):
        v = dot(hot, vb[:, h * 128 : (h + 4) * 128])
        for u in range(4):
            of[:, (h + u) * 128 : (h + u + 1) * 128] = v[:, u * 128 : (u + 1) * 128] * inv[:, h + u : h + u + 1]
    for k in range(16):
        pbuf[k] = of[k * 4 : (k + 1) * 4, :].astype(BF16)
        stbuf[k] = sf[k * 4 : (k + 1) * 4, :]
    for _, q in pools:
        send(stbuf.at[q], rst.at[me], ssem.at[0], ssem.at[1], pool=q)
        send(pbuf.at[q], rp.at[me], psem.at[0], psem.at[1], pool=q)
    rst[me] = stbuf[me]
    rp[me] = pbuf[me]
    settle(rst.at[pl.ds(0, 15)], ssem.at[0], ssem.at[1])
    top = rst[0]
    for s in range(1, 16):
        top = jnp.maximum(top, rst[s])
    tot = jnp.zeros((4, 128), F32)
    for s in range(16):
        e = jnp.exp(rst[s] - top)
        rst[s] = e
        tot = tot + e
    inv = 1.0 / tot
    settle(rp.at[pl.ds(0, 15)], psem.at[0], psem.at[1])

    heads[...] = jnp.zeros((4, 2048), F32)

    @pl.loop(0, 16)
    def _(s):
        w = rst[s] * inv
        for h in range(16):
            cols = slice(h * 128, (h + 1) * 128)
            heads[:, cols] = heads[:, cols] + w[:, h : h + 1] * rp[s, :, cols].astype(F32)

    for g in range(8):
        hs[g] = heads[:, g * 256 : (g + 1) * 256].astype(BF16)
    for _, q in reps:
        send(hs.at[q], hb.at[rp_me], hsem.at[0], hsem.at[1], rep=q)
    hb[rp_me] = hs[rp_me]
    wl[2].wait()
    settle(hb.at[pl.ds(0, 7)], hsem.at[0], hsem.at[1])
    for g in range(8):
        hbf[g * 4 : (g + 1) * 4, :] = hb[g].astype(F32)
    pf[...] = dot(hbf[...].astype(BF16), oproj[...])
    for g in range(8):
        ps[g] = pf[g * 4 : (g + 1) * 4, :].astype(BF16)
    for _, q in reps:
        send(ps.at[q], pr.at[rp_me], osem.at[0], osem.at[1], rep=q)
    pr[rp_me] = ps[rp_me]
    settle(pr.at[pl.ds(0, 7)], osem.at[0], osem.at[1])
    proj = pr[0].astype(F32)
    for g in range(1, 8):
        proj = proj + pr[g].astype(F32)
    proj_out[...] = proj
    res = hid[...].astype(F32) + proj
    ms = jnp.mean(res * res, axis=1, keepdims=True)
    normed = (res * lax.rsqrt(ms + EPS) * gain[...]).astype(BF16)

    nown[...] = normed
    cp = send(nown, npart, nsem.at[0], nsem.at[1], rep=mate)
    settle(gates.at[pl.ds(0, 15)], gsem.at[0], gsem.at[1])
    cp.wait()
    mine = normed.astype(F32)
    theirs = npart[...].astype(F32)
    blk[0:4, :] = jnp.where(c == 0, mine, theirs)
    blk[4:8, :] = jnp.where(c == 0, theirs, mine)
    for t in range(3):
        s = pl.ds(pl.multiple_of(c * 1024 + STARTS[t], 128), WIDTHS[t])
        xs[t][c, x, z, y] = blk[:, s].astype(BF16)

    whole = pl.ds(0, 4)

    def idx(at):
        return tuple(at[a] if not isinstance(at[a], jax.Array) else pl.ds(at[a], 1) for a in "xzy")

    def near(a, d):
        return (coord[a] + d) % 4

    def share(t, at):
        ref = xs[t].at[(c,) + idx(at)]
        send(ref, ref, fsem.at[0, t], fsem.at[1, t], rep=mate)

    for da in STEPS:
        for db in STEPS:
            if da or db:
                for t in range(3):
                    a, b, _ = ORDERS[t]
                    ref = xs[t].at[(c,) + idx(coord)]
                    send(ref, ref, asem.at[t, 4], asem.at[t, da], **peer(**{a: da, b: db}))
    for da in STEPS:
        for t in range(3):
            a, b, w = ORDERS[t]
            some = pl.ds(0, 4 if da else 3)
            settle(xs[t].at[(c,) + idx({a: near(a, -da), b: some, w: coord[w]})], asem.at[t, da])
            ref = xs[t].at[(c,) + idx({a: near(a, -da), b: whole, w: coord[w]})]
            for d in range(1, 4):
                send(ref, ref, bsem.at[t, 0], bsem.at[t, d], **peer(**{w: d}))
    for t in range(3):
        a, b, w = ORDERS[t]
        share(t, {a: whole, b: whole, w: coord[w]})
    for d in (1, 3, 2):
        for t in range(3):
            a, b, w = ORDERS[t]
            at = {a: whole, b: whole, w: near(w, -d)}
            settle(xs[t].at[(c,) + idx(at)], bsem.at[t, d])
            share(t, at)
    for t in range(3):
        a, b, w = ORDERS[t]
        settle(rbs[t].at[pl.ds(0, 15)], asem.at[t, 4])
        settle(xs[t].at[(c,) + idx({a: whole, b: whole, w: pl.ds(0, 3)})], bsem.at[t, 0])
        settle(xs[t].at[c], fsem.at[0, t], fsem.at[1, t])

    for t in range(3):
        for h in range(2):
            s = h * 1024 + STARTS[t]
            v = xs[t][h].astype(F32).reshape(512, WIDTHS[t]).astype(BF16)
            xm[:, s : s + WIDTHS[t]] = v

    for i in range(3, 9):
        wl[i].wait()

    col = xm[pl.ds(pl.multiple_of(me * 32, 32), 32), :]
    ga = dot_nt(col, sg[...])
    ua = dot_nt(col, su[...])
    shin[...] = (ga / (1.0 + jnp.exp(-ga)) * ua).astype(BF16)

    gm = gates[...].reshape(512, 128)
    for lo, hi in ((0, 256), (256, 512), (512, 704)):
        ga = dot_nt(xm[...], wg[lo:hi, :])
        ua = dot_nt(xm[...], wu[lo:hi, :])
        ids = lax.broadcasted_iota(jnp.int32, (128, hi - lo), 0) % 64
        unit = lax.broadcasted_iota(jnp.int32, (128, hi - lo), 1) + lo
        gw = dot(gm, jnp.where(ids == me * 4 + unit // 176, 1.0, 0.0).astype(BF16))
        inner[:, lo:hi] = (ga / (1.0 + jnp.exp(-ga)) * ua * gw).astype(BF16)

    ys = (y0, y1, y2)
    css = (cs0, cs1, cs2)
    crs = (cr0, cr1, cr2)
    cc = []

    def down(t, half):
        wdt = WIDTHS[t]
        cols = pl.ds(pl.multiple_of(half * 1024 + STARTS[t], 128), wdt)
        v = dot(inner[...], wd[:, cols])
        sh = dot(shin[...], sd[:, cols])
        ys[t][...] = v.reshape(4, 4, 4, 8, wdt)
        ys[t][x, z] = ys[t][x, z] + sh.reshape(4, 8, wdt)

    for t in range(3):
        down(t, 1 - c)
        css[t][...] = ys[t][...].astype(BF16)
        cc.append(send(css[t], crs[t], csem.at[0, t], csem.at[1, t], rep=mate))

    sbs = (sb0, sb1, sb2)

    back = (2, 1, 3, 0)
    for t in range(3):
        down(t, c)
        cc[t].wait()
        tot = ys[t][...] + crs[t][...].astype(F32)
        ys[t][...] = tot
        sbs[t][...] = tot.astype(BF16)
        a, b, w = ORDERS[t]
        for da in back:
            for d in range(1, 4):
                src = sbs[t].at[idx({a: near(a, da), b: whole, w: near(w, d)})]
                dst = ras[t].at[(d,) + idx({a: near(a, da), b: whole, w: coord[w] * 0})]
                send(src, dst, dsem.at[t, 4], dsem.at[t, da], **peer(**{w: d}))
    for da in back:
        for t in range(3):
            a, b, w = ORDERS[t]
            at = idx({a: near(a, da), b: whole, w: coord[w] * 0})
            settle(ras[t].at[(pl.ds(1, 3),) + at], dsem.at[t, da])
            v = ys[t][idx({a: near(a, da), b: whole, w: coord[w]})]
            for d in range(1, 4):
                v = v + ras[t][(d,) + at].astype(F32)
            ras[t][(0,) + at] = v.astype(BF16)
            for db in back:
                k = da * 4 + db
                if k:
                    ref = ras[t].at[(0,) + idx({a: near(a, da), b: near(b, db), w: coord[w] * 0})]
                    dst = rbs[t].at[(k,) + (pl.ds(0, 1),) * 3]
                    send(ref, dst, esem.at[0, t], esem.at[1, t], **peer(**{a: da, b: db}))
    for t in range(3):
        a, b, w = ORDERS[t]
        v = ras[t][(0,) + idx({a: coord[a], b: coord[b], w: coord[w] * 0})].astype(F32)
        settle(rbs[t].at[pl.ds(1, 15)], esem.at[0, t], esem.at[1, t])
        settle(ras[t].at[pl.ds(1, 3)], dsem.at[t, 4])
        for k in range(1, 16):
            v = v + rbs[t][k].astype(F32)
        blk[:, STARTS[t] : STARTS[t] + WIDTHS[t]] = v.reshape(8, WIDTHS[t])
    lo, hi = blk[0:4, 0:1024], blk[4:8, 0:1024]
    fs[...] = jnp.where(c == 0, hi, lo).astype(BF16)
    cp = send(fs, fr, lsem.at[0], lsem.at[1], rep=mate)
    own = jnp.where(c == 0, lo, hi)
    cp.wait()
    other = fr[...].astype(F32)
    moe_out[:, 0:1024] = jnp.where(c == 0, own, other)
    moe_out[:, 1024:2048] = jnp.where(c == 0, other, own)


def dma(*shape):
    return pltpu.SemaphoreType.DMA(shape)


def scratch():
    v = pltpu.VMEM
    i32 = jnp.int32
    big = [v((704, 2048), BF16)] * 3 + [v((352, 2048), BF16)] * 3
    out = [v((16, 128, 512), BF16), v((16, 512, 128), BF16), v((49, 576, 128), BF16), v((256, 2048), BF16)]
    out += big + [dma(9), pltpu.SemaphoreType.DMA]
    out += [
        v((4, 24, 128), BF16), v((16, 4, 24, 128), BF16), v((1024, 128), F32), v((512, 128), F32),
        v((5, 1024, 128), F32), v((4, 1024, 128), F32), v((1024, 128), F32), v((1024, 128), F32),
        v((64, 128), i32), v((64, 128), i32), v((128, 640), F32),
        v((64, 2048), BF16), v((64, 2048), F32), v((64, 128), F32), v((16, 4, 2048), BF16),
        v((16, 4, 128), F32), dma(2),
    ]
    out += [
        v((16, 4, 2048), BF16), v((16, 4, 128), F32), v((32, 128), BF16), v((16, 32, 128), BF16), v((4, 2048), F32),
        v((8, 4, 256), BF16), v((8, 4, 256), BF16), v((32, 256), F32), v((32, 2048), F32),
        v((8, 4, 2048), BF16), v((8, 4, 2048), BF16), v((4, 2048), BF16), v((4, 2048), BF16),
        v((8, 2048), F32),
    ]
    out += [v((2, 4, 4, 4, 8, w), BF16) for w in WIDTHS]
    out += [v((512, 2048), BF16), v((512, 704), BF16), v((32, 352), BF16)]
    out += [v((4, 4, 4, 8, w), F32) for w in WIDTHS]
    out += [v((4, 4, 4, 8, w), BF16) for w in WIDTHS] * 3

    def shape(t):
        return tuple(1 if a == ORDERS[t][2] else 4 for a in "xzy") + (8, WIDTHS[t])

    out += [v((4,) + shape(t), BF16) for t in range(3)]
    out += [v((16, 1, 1, 1, 8, w), BF16) for w in WIDTHS]
    out += [v((4, 1024), BF16), v((4, 1024), BF16)]
    out += [
        dma(2), dma(2), dma(2), dma(2), dma(2), dma(2),
        dma(3, 5), dma(3, 4), dma(2, 3), dma(2, 3), dma(3, 5), dma(2, 3), dma(2),
    ]
    return out


def params(cid):
    return pltpu.CompilerParams(vmem_limit_bytes=LIMIT, collective_id=cid, has_side_effects=True)


def call(q, table, lens, new, hid, gain, routes, gates, *weights):
    sds = jax.ShapeDtypeStruct
    return pl.pallas_call(
        layer,
        out_shape=(sds((4, 2048), F32), sds((4, 2048), F32)),
        in_specs=[VM] * 8 + [HBM] * 10,
        out_specs=(VM, VM),
        scratch_shapes=scratch(),
        compiler_params=params(0),
        name="layer",
    )(q, table, lens, new, hid, gain, routes, gates, *weights)


def shards(
    hidden,
    queries,
    new_kv,
    kv_cache,
    block_table,
    seq_lens,
    w_uk,
    w_uv,
    o_proj,
    norm_gain,
    routes,
    gate_weights,
    w_gate,
    w_up,
    w_down,
    shared_gate,
    shared_up,
    shared_down,
):
    wide = lambda w: jnp.swapaxes(w, -1, -2)
    flat = lambda w: w.reshape(-1, w.shape[-1])
    proj, moe = call(
        queries[0], block_table[0], seq_lens, new_kv[0], hidden[0], norm_gain[None],
        routes[0].T, gate_weights[0].T,
        w_uk, w_uv, wide(kv_cache[0]), o_proj, flat(wide(w_gate)), flat(wide(w_up)), flat(w_down),
        wide(shared_gate), wide(shared_up), shared_down,
    )
    layer_out = (hidden[0].astype(F32) + proj + moe).astype(BF16)
    return proj.astype(BF16)[None], layer_out[None]


def solution(mesh):
    placed = (
        P("rep", "pool", None),
        P("rep", "pool", None, None),
        P("rep", "pool", None),
        P("rep", "pool", None, None),
        P("rep", None, None),
        P("rep", None),
        P(),
        P(),
        P("rep", None),
        P(),
        P("pool", None, None, None),
        P("pool", None, None, None),
        P("pool", None, "rep"),
        P("pool", None, "rep"),
        P("pool", "rep", None),
        P(None, "rep"),
        P(None, "rep"),
        P("rep", None),
    )
    return jax.shard_map(
        shards,
        mesh=mesh,
        in_specs=placed,
        out_specs=(P("rep", "pool", None), P("rep", "pool", None)),
        check_vma=False,
    )
```

```python
import functools

import jax
import jax.numpy as jnp
from jax import lax
from jax.experimental import pallas as pl
from jax.experimental.pallas import tpu as pltpu
from jax.sharding import PartitionSpec as P

F32 = jnp.float32
BF16 = jnp.bfloat16
NEG = -1e30
EPS = 1e-06
NX = 4
MESH = pl.DeviceIdType.MESH
VM = pl.BlockSpec(memory_space=pltpu.VMEM)
HBM = pl.BlockSpec(memory_space=pl.ANY)
SM = pl.BlockSpec(memory_space=pltpu.SMEM)
NT = (((1,), (1,)), ((), ()))
LIMIT = 60 * 1024 * 1024


def dot(a, b):
    return jnp.dot(a, b, preferred_element_type=F32)


def dot_nt(a, b):
    return lax.dot_general(a, b, NT, preferred_element_type=F32)


def place():
    p = lax.axis_index("pool")
    r = lax.axis_index("rep")
    return p // NX, p % NX, r // 2, r % 2


def pool_peers(x, z):
    out = []
    for d in range(1, 16):
        dx, dz = d // 4, d % 4
        out.append((d, ((x + dx) % 4) * 4 + (z + dz) % 4))
    return out


def rep_peers(y, c):
    out = []
    for d in range(1, 8):
        dy, dc = d // 2, d % 2
        out.append((d, ((y + dy) % 4) * 2 + (c + dc) % 2))
    return out


def send(src, dst, ssem, rsem, pool=None, rep=None):
    dev = {}
    if pool is not None:
        dev["pool"] = pool
    if rep is not None:
        dev["rep"] = rep
    cp = pltpu.make_async_remote_copy(
        src_ref=src, dst_ref=dst, send_sem=ssem, recv_sem=rsem, device_id=dev, device_id_type=MESH
    )
    cp.start()
    return cp


def settle(ref, *sems):
    for sem in sems:
        pltpu.make_async_copy(ref, ref, sem).wait()


def hail(devices):
    bar = pltpu.get_barrier_semaphore()
    for dev in devices:
        pl.semaphore_signal(bar, inc=1, device_id=dev, device_id_type=MESH)


def meet(devices):
    pl.semaphore_wait(pltpu.get_barrier_semaphore(), len(devices))


WIDTHS = (384, 384, 256)
STARTS = (0, 384, 768)
ORDERS = (("x", "z", "y"), ("z", "y", "x"), ("y", "x", "z"))
STEPS = (0, 1, 3, 2)
AX = {"x": 0, "z": 1, "y": 2}


def layer(
    q_in, table_in, len_in, new_in, hid, gain, routes_in, weights_in,
    wuk_h, wuv_h, cache, oproj_h, wg_h, wu_h, wd_h, sg_h, su_h, sd_h,
    proj_out, moe_out,
    wuk, wuv, kv, oproj, wg, wu, wd, sg, su, sd, wsem, kvsem,
    qp, qg, qf, qr, fq, nb, mb, db, mrow, meta_v, wide, vb, of, sf, pbuf, stbuf, qsem,
    rp, rst, gates_own, gates, heads, hs, hb, hbf, pf, ps, pr, nown, npart, blk,
    x0, x1, x2, xm, gws, inner, shin, y0, y1, y2, cs0, cs1, cs2, cr0, cr1, cr2,
    sb0, sb1, sb2, ra0, ra1, ra2, rb0, rb1, rb2, fs, fr,
    psem, ssem, gsem, hsem, osem, nsem, asem, bsem, fsem, csem, dsem, esem, lsem,
):
    x, z, y, c = place()
    me = x * 4 + z
    rp_me = y * 2 + c
    coord = {"x": x, "z": z, "y": y}
    pools = pool_peers(x, z)
    reps = rep_peers(y, c)
    mate = y * 2 + 1 - c
    xs = (x0, x1, x2)
    ras, rbs = (ra0, ra1, ra2), (rb0, rb1, rb2)
    pages, rows = 48, 64
    scale = 192 ** (-0.5)

    def load(h, v, sem):
        cp = pltpu.make_async_copy(h, v, sem)
        cp.start()
        return cp

    wl = {0: load(wuk_h, wuk, wsem.at[0])}
    kl = load(cache, kv.at[pl.ds(0, pages)], kvsem)

    def peer(**over):
        at = {a: (coord[a] + over.get(a, 0)) % 4 for a in "xzy"}
        return {"pool": at["x"] * 4 + at["z"], "rep": at["y"] * 2 + c}

    def more():
        for i, (h, v) in enumerate(
            ((wuv_h, wuv), (oproj_h, oproj), (sg_h, sg), (su_h, su), (sd_h, sd), (wg_h, wg), (wu_h, wu), (wd_h, wd))
        ):
            wl[i + 1] = load(h, v, wsem.at[i + 1])

    known = (
        [{"pool": q, "rep": rp_me} for _, q in pools]
        + [{"pool": me, "rep": q} for _, q in reps]
        + [peer(**{a: da, "y": dy}) for a in "xz" for da in range(1, 4) for dy in range(1, 4)]
    )
    hail(known)
    for k in range(4):
        v = q_in[k].astype(F32)
        qp[k, 0:16, :] = v[:, 0:128].astype(BF16)
        qp[k, 16:24, :] = jnp.concatenate([v[0:8, 128:192], v[8:16, 128:192]], axis=1).astype(BF16)
    sub = lax.broadcasted_iota(jnp.int32, (64, 128), 0)
    lane = lax.broadcasted_iota(jnp.int32, (64, 128), 1)
    lens = jnp.broadcast_to(len_in[...], (64, 64))
    diag = lax.broadcasted_iota(jnp.int32, (64, 64), 0) == lax.broadcasted_iota(jnp.int32, (64, 64), 1)
    lens = jnp.sum(jnp.where(diag, lens, 0), axis=1, keepdims=True)
    filled = jnp.clip(lens - lane * 128, 0, 128)
    code = sub * 256 + filled
    local = jnp.where(filled > 0, table_in[...] - me * pages, -1)
    for i in range(pages):
        mrow[i : i + 1, :] = jnp.sum(jnp.where(local == i, code, 0), axis=0, keepdims=True)
    mrow[pages:rows, :] = jnp.zeros((rows - pages, 128), jnp.int32)
    codes = jnp.broadcast_to(jnp.sum(mrow[...], axis=1, keepdims=True), (rows, 128))
    meta_v[...] = codes % 256
    virtual = (sub >= pages) & (sub < pages + 4)
    owner = jnp.where(virtual, me * 4 + sub - pages, codes // 256)

    ids64 = lax.broadcasted_iota(jnp.int32, (64, 8), 0)
    row32 = lax.broadcasted_iota(jnp.int32, (32, 8), 0)
    col8 = lax.broadcasted_iota(jnp.int32, (32, 8), 1)
    coarse = jnp.zeros((32, 64), F32)
    fine = coarse
    for q in range(4):
        v = jnp.zeros((64, 8), F32)
        for k in range(6):
            v = v + jnp.where(routes_in[k, q : q + 1, :] == ids64, weights_in[k, q : q + 1, :], 0.0)
        high = v.astype(BF16)
        low = (v - high.astype(F32)).astype(BF16)
        at = jnp.where(row32 == col8 * 4 + q, 1.0, 0.0).astype(BF16)
        coarse = coarse + dot_nt(at, high)
        fine = fine + dot_nt(at, low)
    gates_own[...] = jnp.concatenate([coarse, fine], axis=1).astype(BF16)

    meet(known)

    for _, q in pools:
        send(qp, qg.at[me], qsem.at[0], qsem.at[1], pool=q)
    qg[me] = qp[...]

    wide[...] = jnp.zeros((128, 640), F32)
    wide[0:4, 0:576] = new_in[...].astype(F32)
    for t in range(5):
        n = 64 if t == 4 else 128
        kv[pages, t * 128 : t * 128 + n, :] = wide[:, t * 128 : (t + 1) * 128].T[0:n, :].astype(BF16)
    mb[pages * 16 + 64 :, :] = jnp.full(((rows - pages - 4) * 16, 128), NEG, F32)
    db[pages * 16 + 64 :, :] = jnp.zeros(((rows - pages - 4) * 16, 128), F32)
    for t in range(4):
        nb[t, pages * 16 + 64 :, :] = jnp.zeros(((rows - pages - 4) * 16, 128), F32)

    settle(qg.at[pl.ds(0, 15)], qsem.at[0], qsem.at[1])
    for _, q in pools:
        send(gates_own, gates.at[me], gsem.at[0], gsem.at[1], pool=q)
    gates[me] = gates_own[...]
    wl[0].wait()

    @pl.loop(0, 64, unroll=4)
    def _(j):
        v = qg[j // 4, j % 4].astype(F32)
        qf[pl.ds(pl.multiple_of(j * 16, 16), 16), :] = v[0:16]
        qr[pl.ds(pl.multiple_of(j * 8, 8), 8), :] = v[16:24]

    hot = jnp.where(lane == owner, 1.0, 0.0)
    pick = hot[:, 0:64].astype(BF16)
    for h in range(16):
        s = pl.ds(h, 64, stride=16)
        a = dot(dot(pick, qf[s, :].astype(BF16)).astype(BF16), wuk[h]) * scale
        for t in range(4):
            fq[t, s, :] = a[:, t * 128 : (t + 1) * 128]
        b = dot(pick, qr[pl.ds(h % 8, 64, stride=8), :].astype(BF16)) * scale
        if h >= 8:
            b = jnp.concatenate([b[:, 64:128], b[:, 0:64]], axis=1)
        fq[4, s, :] = b
    more()
    group = lax.broadcasted_iota(jnp.int32, (32, 256), 0) // 16
    spot = lax.broadcasted_iota(jnp.int32, (32, 256), 1) - group * 128

    def pair(i, one, two, lo, hi):
        s = pl.ds(pl.multiple_of(i * 16, 32), 32)
        qa = jnp.concatenate([fq[t, s, :] for t in range(4)], axis=1).astype(BF16)
        qb = fq[4, s, :][:, 0:64].astype(BF16)
        kk = jnp.concatenate([kv[one], kv[two]], axis=1)
        v = dot(qa, kk[0:512, :]) + dot(qb, kk[512:576, :])
        ok = (spot >= lo) & (spot < hi)
        v = jnp.where(ok, v, NEG)
        m = jnp.max(v, axis=1, keepdims=True)
        w = jnp.where(ok, jnp.exp(v - m), 0.0).astype(BF16)
        den = jnp.sum(w.astype(F32), axis=1, keepdims=True)
        num = dot_nt(w, kk[0:512, :])
        mb[s, :] = jnp.broadcast_to(m, (32, 128))
        db[s, :] = jnp.broadcast_to(den, (32, 128))
        for t in range(4):
            nb[t, s, :] = num[:, t * 128 : (t + 1) * 128]

    for k in (0, 2):
        pair(pages + k, pages, pages, group + k, group + k + 1)
    kl.wait()

    @pl.loop(0, pages // 16)
    def _(g):
        for u in range(0, 16, 2):
            i = g * 16 + u
            hi = [jnp.broadcast_to(meta_v[pl.ds(i + n, 1), :], (16, 128)) for n in range(2)]
            hi = jnp.concatenate(hi, axis=0)
            pair(i, i, i + 1, 0, jnp.concatenate([hi, hi], axis=1))


    m = jnp.full((rows, 128), NEG, F32)
    d = jnp.zeros((rows, 128), F32)
    for h in range(16):
        s = pl.ds(h, rows, stride=16)
        m = jnp.where(lane == h, mb[s, :], m)
        d = jnp.where(lane == h, db[s, :], d)
    sf[...] = m
    meta_v[...] = owner
    lp = jnp.full((rows, 128), NEG, F32)
    lr = lp
    for i in range(pages + 4):
        o = meta_v[i : i + 1, :]
        row = sf[i : i + 1, :]
        lp = jnp.maximum(lp, jnp.where(owner == o, row, NEG))
        lr = jnp.maximum(lr, jnp.where(sub == o, row, NEG))
    e = jnp.exp(m - lp)
    hot = hot.T[0:64, :]
    rd = lax.dot_general(
        hot, e * d, (((1,), (0,)), ((), ())), preferred_element_type=F32, precision=lax.Precision.HIGHEST
    )
    wl[1].wait()
    for h in range(16):
        s = pl.ds(h, rows, stride=16)
        a = jnp.concatenate([nb[t, s, :] for t in range(4)], axis=1).astype(BF16)
        vb[:, h * 128 : (h + 1) * 128] = (dot(a, wuv[h]) * e[:, h : h + 1]).astype(BF16)
    full = rd > 0.0
    safe = jnp.where(full, rd, 1.0)
    inv = 1.0 / safe
    sf[...] = jnp.where(full, lr + jnp.log(safe), NEG)
    hot = hot.astype(BF16)
    for h in range(0, 16, 4):
        v = dot(hot, vb[:, h * 128 : (h + 4) * 128])
        for u in range(4):
            of[:, (h + u) * 128 : (h + u + 1) * 128] = v[:, u * 128 : (u + 1) * 128] * inv[:, h + u : h + u + 1]
    for k in range(16):
        pbuf[k] = of[k * 4 : (k + 1) * 4, :].astype(BF16)
        stbuf[k] = sf[k * 4 : (k + 1) * 4, :]
    for _, q in pools:
        send(stbuf.at[q], rst.at[me], ssem.at[0], ssem.at[1], pool=q)
        send(pbuf.at[q], rp.at[me], psem.at[0], psem.at[1], pool=q)
    rst[me] = stbuf[me]
    rp[me] = pbuf[me]
    settle(rst.at[pl.ds(0, 15)], ssem.at[0], ssem.at[1])
    top = rst[0]
    for s in range(1, 16):
        top = jnp.maximum(top, rst[s])
    tot = jnp.zeros((4, 128), F32)
    for s in range(16):
        e = jnp.exp(rst[s] - top)
        rst[s] = e
        tot = tot + e
    inv = 1.0 / tot
    shares = [rst[s] * inv for s in range(16)]
    settle(rp.at[pl.ds(0, 15)], psem.at[0], psem.at[1])

    for h in range(16):
        cols = slice(h * 128, (h + 1) * 128)
        v = jnp.zeros((4, 128), F32)
        for s in range(16):
            v = v + shares[s][:, h : h + 1] * rp[s, :, cols].astype(F32)
        heads[:, cols] = v

    for g in range(8):
        hs[g] = heads[:, g * 256 : (g + 1) * 256].astype(BF16)
    for _, q in reps:
        send(hs.at[q], hb.at[rp_me], hsem.at[0], hsem.at[1], rep=q)
    hb[rp_me] = hs[rp_me]
    wl[2].wait()
    settle(hb.at[pl.ds(0, 7)], hsem.at[0], hsem.at[1])
    for g in range(8):
        hbf[g * 4 : (g + 1) * 4, :] = hb[g].astype(F32)
    pf[...] = dot(hbf[...].astype(BF16), oproj[...])
    for g in range(8):
        ps[g] = pf[g * 4 : (g + 1) * 4, :].astype(BF16)
    for _, q in reps:
        send(ps.at[q], pr.at[rp_me], osem.at[0], osem.at[1], rep=q)
    pr[rp_me] = ps[rp_me]
    settle(pr.at[pl.ds(0, 7)], osem.at[0], osem.at[1])
    proj = pr[0].astype(F32)
    for g in range(1, 8):
        proj = proj + pr[g].astype(F32)
    proj_out[...] = proj
    res = hid[...].astype(F32) + proj
    ms = jnp.mean(res * res, axis=1, keepdims=True)
    normed = (res * lax.rsqrt(ms + EPS) * gain[...]).astype(BF16)

    nown[...] = normed
    cp = send(nown, npart, nsem.at[0], nsem.at[1], rep=mate)
    settle(gates.at[pl.ds(0, 15)], gsem.at[0], gsem.at[1])
    cp.wait()
    mine = normed.astype(F32)
    theirs = npart[...].astype(F32)
    blk[0:4, :] = jnp.where(c == 0, mine, theirs)
    blk[4:8, :] = jnp.where(c == 0, theirs, mine)
    for t in range(3):
        s = pl.ds(pl.multiple_of(c * 1024 + STARTS[t], 128), WIDTHS[t])
        xs[t][c, x, z, y] = blk[:, s].astype(BF16)

    whole = pl.ds(0, 4)

    def idx(at):
        return tuple(at[a] if not isinstance(at[a], jax.Array) else pl.ds(at[a], 1) for a in "xzy")

    def near(a, d):
        return (coord[a] + d) % 4

    def share(t, at):
        ref = xs[t].at[(c,) + idx(at)]
        send(ref, ref, fsem.at[0, t], fsem.at[1, t], rep=mate)

    for da in STEPS:
        for db in STEPS:
            if da or db:
                for t in range(3):
                    a, b, _ = ORDERS[t]
                    ref = xs[t].at[(c,) + idx(coord)]
                    send(ref, ref, asem.at[t, 4], asem.at[t, da], **peer(**{a: da, b: db}))
    gm = gates[...].reshape(512, 128)
    for lo, hi in ((0, 256), (256, 512), (512, 704)):
        ids = lax.broadcasted_iota(jnp.int32, (128, hi - lo), 0) % 64
        unit = lax.broadcasted_iota(jnp.int32, (128, hi - lo), 1) + lo
        gws[:, lo:hi] = dot(gm, jnp.where(ids == me * 4 + unit // 176, 1.0, 0.0).astype(BF16))
    for da in STEPS:
        for t in range(3):
            a, b, w = ORDERS[t]
            some = pl.ds(0, 4 if da else 3)
            settle(xs[t].at[(c,) + idx({a: near(a, -da), b: some, w: coord[w]})], asem.at[t, da])
            ref = xs[t].at[(c,) + idx({a: near(a, -da), b: whole, w: coord[w]})]
            for d in range(1, 4):
                send(ref, ref, bsem.at[t, 0], bsem.at[t, d], **peer(**{w: d}))
    for t in range(3):
        a, b, w = ORDERS[t]
        share(t, {a: whole, b: whole, w: coord[w]})
    for d in (1, 3, 2):
        for t in range(3):
            a, b, w = ORDERS[t]
            at = {a: whole, b: whole, w: near(w, -d)}
            settle(xs[t].at[(c,) + idx(at)], bsem.at[t, d])
            share(t, at)
    for t in range(3):
        a, b, w = ORDERS[t]
        settle(rbs[t].at[pl.ds(0, 15)], asem.at[t, 4])
        settle(xs[t].at[(c,) + idx({a: whole, b: whole, w: pl.ds(0, 3)})], bsem.at[t, 0])
        settle(xs[t].at[c], fsem.at[0, t], fsem.at[1, t])

    for t in range(3):
        for h in range(2):
            s = h * 1024 + STARTS[t]
            v = xs[t][h].astype(F32).reshape(512, WIDTHS[t]).astype(BF16)
            xm[:, s : s + WIDTHS[t]] = v

    for i in range(3, 9):
        wl[i].wait()

    col = xm[pl.ds(pl.multiple_of(me * 32, 32), 32), :]
    ga = dot_nt(col, sg[...])
    ua = dot_nt(col, su[...])
    shin[...] = (ga / (1.0 + jnp.exp(-ga)) * ua).astype(BF16)

    for lo, hi in ((0, 256), (256, 512), (512, 704)):
        ga = dot_nt(xm[...], wg[lo:hi, :])
        ua = dot_nt(xm[...], wu[lo:hi, :])
        inner[:, lo:hi] = (ga / (1.0 + jnp.exp(-ga)) * ua * gws[:, lo:hi]).astype(BF16)

    ys = (y0, y1, y2)
    css = (cs0, cs1, cs2)
    crs = (cr0, cr1, cr2)
    cc = []

    def down(t, half):
        wdt = WIDTHS[t]
        cols = pl.ds(pl.multiple_of(half * 1024 + STARTS[t], 128), wdt)
        v = dot(inner[...], wd[:, cols])
        sh = dot(shin[...], sd[:, cols])
        ys[t][...] = v.reshape(4, 4, 4, 8, wdt)
        ys[t][x, z] = ys[t][x, z] + sh.reshape(4, 8, wdt)

    for t in range(3):
        down(t, 1 - c)
        css[t][...] = ys[t][...].astype(BF16)
        cc.append(send(css[t], crs[t], csem.at[0, t], csem.at[1, t], rep=mate))

    sbs = (sb0, sb1, sb2)

    back = (2, 1, 3, 0)
    for t in range(3):
        down(t, c)
        cc[t].wait()
        tot = ys[t][...] + crs[t][...].astype(F32)
        ys[t][...] = tot
        sbs[t][...] = tot.astype(BF16)
        a, b, w = ORDERS[t]
        for da in back:
            for d in range(1, 4):
                src = sbs[t].at[idx({a: near(a, da), b: whole, w: near(w, d)})]
                dst = ras[t].at[(d,) + idx({a: near(a, da), b: whole, w: coord[w] * 0})]
                send(src, dst, dsem.at[t, 4], dsem.at[t, da], **peer(**{w: d}))
    for da in back:
        for t in range(3):
            a, b, w = ORDERS[t]
            at = idx({a: near(a, da), b: whole, w: coord[w] * 0})
            settle(ras[t].at[(pl.ds(1, 3),) + at], dsem.at[t, da])
            v = ys[t][idx({a: near(a, da), b: whole, w: coord[w]})]
            for d in range(1, 4):
                v = v + ras[t][(d,) + at].astype(F32)
            ras[t][(0,) + at] = v.astype(BF16)
            for db in back:
                k = da * 4 + db
                if k:
                    ref = ras[t].at[(0,) + idx({a: near(a, da), b: near(b, db), w: coord[w] * 0})]
                    dst = rbs[t].at[(k,) + (pl.ds(0, 1),) * 3]
                    send(ref, dst, esem.at[0, t], esem.at[1, t], **peer(**{a: da, b: db}))
    for t in range(3):
        a, b, w = ORDERS[t]
        v = ras[t][(0,) + idx({a: coord[a], b: coord[b], w: coord[w] * 0})].astype(F32)
        settle(rbs[t].at[pl.ds(1, 15)], esem.at[0, t], esem.at[1, t])
        settle(ras[t].at[pl.ds(1, 3)], dsem.at[t, 4])
        for k in range(1, 16):
            v = v + rbs[t][k].astype(F32)
        blk[:, STARTS[t] : STARTS[t] + WIDTHS[t]] = v.reshape(8, WIDTHS[t])
    lo, hi = blk[0:4, 0:1024], blk[4:8, 0:1024]
    fs[...] = jnp.where(c == 0, hi, lo).astype(BF16)
    cp = send(fs, fr, lsem.at[0], lsem.at[1], rep=mate)
    own = jnp.where(c == 0, lo, hi)
    cp.wait()
    other = fr[...].astype(F32)
    moe_out[:, 0:1024] = jnp.where(c == 0, own, other)
    moe_out[:, 1024:2048] = jnp.where(c == 0, other, own)


def dma(*shape):
    return pltpu.SemaphoreType.DMA(shape)


def scratch():
    v = pltpu.VMEM
    i32 = jnp.int32
    big = [v((704, 2048), BF16)] * 3 + [v((352, 2048), BF16)] * 3
    out = [v((16, 128, 512), BF16), v((16, 512, 128), BF16), v((49, 576, 128), BF16), v((256, 2048), BF16)]
    out += big + [dma(9), pltpu.SemaphoreType.DMA]
    out += [
        v((4, 24, 128), BF16), v((16, 4, 24, 128), BF16), v((1024, 128), F32), v((512, 128), F32),
        v((5, 1024, 128), F32), v((4, 1024, 128), F32), v((1024, 128), F32), v((1024, 128), F32),
        v((64, 128), i32), v((64, 128), i32), v((128, 640), F32),
        v((64, 2048), BF16), v((64, 2048), F32), v((64, 128), F32), v((16, 4, 2048), BF16),
        v((16, 4, 128), F32), dma(2),
    ]
    out += [
        v((16, 4, 2048), BF16), v((16, 4, 128), F32), v((32, 128), BF16), v((16, 32, 128), BF16), v((4, 2048), F32),
        v((8, 4, 256), BF16), v((8, 4, 256), BF16), v((32, 256), F32), v((32, 2048), F32),
        v((8, 4, 2048), BF16), v((8, 4, 2048), BF16), v((4, 2048), BF16), v((4, 2048), BF16),
        v((8, 2048), F32),
    ]
    out += [v((2, 4, 4, 4, 8, w), BF16) for w in WIDTHS]
    out += [v((512, 2048), BF16), v((512, 704), F32), v((512, 704), BF16), v((32, 352), BF16)]
    out += [v((4, 4, 4, 8, w), F32) for w in WIDTHS]
    out += [v((4, 4, 4, 8, w), BF16) for w in WIDTHS] * 3

    def shape(t):
        return tuple(1 if a == ORDERS[t][2] else 4 for a in "xzy") + (8, WIDTHS[t])

    out += [v((4,) + shape(t), BF16) for t in range(3)]
    out += [v((16, 1, 1, 1, 8, w), BF16) for w in WIDTHS]
    out += [v((4, 1024), BF16), v((4, 1024), BF16)]
    out += [
        dma(2), dma(2), dma(2), dma(2), dma(2), dma(2),
        dma(3, 5), dma(3, 4), dma(2, 3), dma(2, 3), dma(3, 5), dma(2, 3), dma(2),
    ]
    return out


def params(cid):
    return pltpu.CompilerParams(vmem_limit_bytes=LIMIT, collective_id=cid, has_side_effects=True)


def call(q, table, lens, new, hid, gain, routes, gates, *weights):
    sds = jax.ShapeDtypeStruct
    return pl.pallas_call(
        layer,
        out_shape=(sds((4, 2048), F32), sds((4, 2048), F32)),
        in_specs=[VM] * 8 + [HBM] * 10,
        out_specs=(VM, VM),
        scratch_shapes=scratch(),
        compiler_params=params(0),
        name="layer",
    )(q, table, lens, new, hid, gain, routes, gates, *weights)


def shards(
    hidden,
    queries,
    new_kv,
    kv_cache,
    block_table,
    seq_lens,
    w_uk,
    w_uv,
    o_proj,
    norm_gain,
    routes,
    gate_weights,
    w_gate,
    w_up,
    w_down,
    shared_gate,
    shared_up,
    shared_down,
):
    wide = lambda w: jnp.swapaxes(w, -1, -2)
    flat = lambda w: w.reshape(-1, w.shape[-1])
    proj, moe = call(
        queries[0], block_table[0], seq_lens, new_kv[0], hidden[0], norm_gain[None],
        routes[0].T, gate_weights[0].T,
        w_uk, w_uv, wide(kv_cache[0]), o_proj, flat(wide(w_gate)), flat(wide(w_up)), flat(w_down),
        wide(shared_gate), wide(shared_up), shared_down,
    )
    layer_out = (hidden[0].astype(F32) + proj + moe).astype(BF16)
    return proj.astype(BF16)[None], layer_out[None]


def solution(mesh):
    placed = (
        P("rep", "pool", None),
        P("rep", "pool", None, None),
        P("rep", "pool", None),
        P("rep", "pool", None, None),
        P("rep", None, None),
        P("rep", None),
        P(),
        P(),
        P("rep", None),
        P(),
        P("pool", None, None, None),
        P("pool", None, None, None),
        P("pool", None, "rep"),
        P("pool", None, "rep"),
        P("pool", "rep", None),
        P(None, "rep"),
        P(None, "rep"),
        P("rep", None),
    )
    return jax.shard_map(
        shards,
        mesh=mesh,
        in_specs=placed,
        out_specs=(P("rep", "pool", None), P("rep", "pool", None)),
        check_vma=False,
    )
```

```python
import functools

import jax
import jax.numpy as jnp
from jax import lax
from jax.experimental import pallas as pl
from jax.experimental.pallas import tpu as pltpu
from jax.sharding import PartitionSpec as P

F32 = jnp.float32
BF16 = jnp.bfloat16
NEG = -1e30
EPS = 1e-06
NX = 4
MESH = pl.DeviceIdType.MESH
VM = pl.BlockSpec(memory_space=pltpu.VMEM)
HBM = pl.BlockSpec(memory_space=pl.ANY)
SM = pl.BlockSpec(memory_space=pltpu.SMEM)
NT = (((1,), (1,)), ((), ()))
LIMIT = 60 * 1024 * 1024


def dot(a, b):
    return jnp.dot(a, b, preferred_element_type=F32)


def dot_nt(a, b):
    return lax.dot_general(a, b, NT, preferred_element_type=F32)


def place():
    p = lax.axis_index("pool")
    r = lax.axis_index("rep")
    return p // NX, p % NX, r // 2, r % 2


def pool_peers(x, z):
    out = []
    for d in range(1, 16):
        dx, dz = d // 4, d % 4
        out.append((d, ((x + dx) % 4) * 4 + (z + dz) % 4))
    return out


def rep_peers(y, c):
    out = []
    for d in range(1, 8):
        dy, dc = d // 2, d % 2
        out.append((d, ((y + dy) % 4) * 2 + (c + dc) % 2))
    return out


def send(src, dst, ssem, rsem, pool=None, rep=None):
    dev = {}
    if pool is not None:
        dev["pool"] = pool
    if rep is not None:
        dev["rep"] = rep
    cp = pltpu.make_async_remote_copy(
        src_ref=src, dst_ref=dst, send_sem=ssem, recv_sem=rsem, device_id=dev, device_id_type=MESH
    )
    cp.start()
    return cp


def settle(ref, *sems):
    for sem in sems:
        pltpu.make_async_copy(ref, ref, sem).wait()


def hail(devices):
    bar = pltpu.get_barrier_semaphore()
    for dev in devices:
        pl.semaphore_signal(bar, inc=1, device_id=dev, device_id_type=MESH)


def meet(devices):
    pl.semaphore_wait(pltpu.get_barrier_semaphore(), len(devices))


WIDTHS = (384, 384, 256)
STARTS = (0, 384, 768)
ORDERS = (("x", "z", "y"), ("z", "y", "x"), ("y", "x", "z"))
STEPS = (0, 1, 3, 2)
AX = {"x": 0, "z": 1, "y": 2}


def layer(
    q_in, table_in, len_in, new_in, routes_in, weights_in, hid_h, gain_h,
    wuk_h, wuv_h, cache, oproj_h, wg_h, wu_h, wd_h, sg_h, su_h, sd_h,
    proj_out, moe_out,
    wuk, wuv, kv, oproj, wg, wu, wd, sg, su, sd, hid, gain, wsem, kvsem,
    qp, qg, qf, qr, fq, nb, mb, db, mrow, meta_v, wide, vb, of, sf, pbuf, stbuf, qsem,
    rp, rst, gates_own, gates, heads, hs, hb, hbf, pf, ps, pr, nown, npart, blk,
    x0, x1, x2, xm, gws, inner, shin, y0, y1, y2, cs0, cs1, cs2, cr0, cr1, cr2,
    sb0, sb1, sb2, ra0, ra1, ra2, rb0, rb1, rb2, fs, fr,
    psem, ssem, gsem, hsem, osem, nsem, asem, bsem, fsem, csem, dsem, esem, lsem,
):
    x, z, y, c = place()
    me = x * 4 + z
    rp_me = y * 2 + c
    coord = {"x": x, "z": z, "y": y}
    pools = pool_peers(x, z)
    reps = rep_peers(y, c)
    mate = y * 2 + 1 - c
    xs = (x0, x1, x2)
    ras, rbs = (ra0, ra1, ra2), (rb0, rb1, rb2)
    pages, rows = 48, 64
    scale = 192 ** (-0.5)

    def load(h, v, sem):
        cp = pltpu.make_async_copy(h, v, sem)
        cp.start()
        return cp

    wl = {0: load(wuk_h, wuk, wsem.at[0])}
    kl = load(cache, kv.at[pl.ds(0, pages)], kvsem)

    def peer(**over):
        at = {a: (coord[a] + over.get(a, 0)) % 4 for a in "xzy"}
        return {"pool": at["x"] * 4 + at["z"], "rep": at["y"] * 2 + c}

    def more():
        for i, (h, v) in enumerate(
            ((wuv_h, wuv), (oproj_h, oproj), (sg_h, sg), (su_h, su), (sd_h, sd), (wg_h, wg), (wu_h, wu), (wd_h, wd),
             (hid_h, hid), (gain_h, gain))
        ):
            wl[i + 1] = load(h, v, wsem.at[i + 1])

    known = (
        [{"pool": q, "rep": rp_me} for _, q in pools]
        + [{"pool": me, "rep": q} for _, q in reps]
        + [peer(**{a: da, "y": dy}) for a in "xz" for da in range(1, 4) for dy in range(1, 4)]
    )
    hail(known)
    for k in range(4):
        v = q_in[k].astype(F32)
        qp[k, 0:16, :] = v[:, 0:128].astype(BF16)
        qp[k, 16:24, :] = jnp.concatenate([v[0:8, 128:192], v[8:16, 128:192]], axis=1).astype(BF16)
    sub = lax.broadcasted_iota(jnp.int32, (64, 128), 0)
    lane = lax.broadcasted_iota(jnp.int32, (64, 128), 1)
    lens = jnp.broadcast_to(len_in[...], (64, 64))
    diag = lax.broadcasted_iota(jnp.int32, (64, 64), 0) == lax.broadcasted_iota(jnp.int32, (64, 64), 1)
    lens = jnp.sum(jnp.where(diag, lens, 0), axis=1, keepdims=True)
    filled = jnp.clip(lens - lane * 128, 0, 128)
    code = sub * 256 + filled
    local = jnp.where(filled > 0, table_in[...] - me * pages, -1)
    for i in range(pages):
        mrow[i : i + 1, :] = jnp.sum(jnp.where(local == i, code, 0), axis=0, keepdims=True)
    mrow[pages:rows, :] = jnp.zeros((rows - pages, 128), jnp.int32)
    codes = jnp.broadcast_to(jnp.sum(mrow[...], axis=1, keepdims=True), (rows, 128))
    meta_v[...] = codes % 256
    virtual = (sub >= pages) & (sub < pages + 4)
    owner = jnp.where(virtual, me * 4 + sub - pages, codes // 256)

    ids64 = lax.broadcasted_iota(jnp.int32, (64, 8), 0)
    row32 = lax.broadcasted_iota(jnp.int32, (32, 8), 0)
    col8 = lax.broadcasted_iota(jnp.int32, (32, 8), 1)
    coarse = jnp.zeros((32, 64), F32)
    fine = coarse
    for q in range(4):
        v = jnp.zeros((64, 8), F32)
        for k in range(6):
            v = v + jnp.where(routes_in[k, q : q + 1, :] == ids64, weights_in[k, q : q + 1, :], 0.0)
        high = v.astype(BF16)
        low = (v - high.astype(F32)).astype(BF16)
        at = jnp.where(row32 == col8 * 4 + q, 1.0, 0.0).astype(BF16)
        coarse = coarse + dot_nt(at, high)
        fine = fine + dot_nt(at, low)
    gates_own[...] = jnp.concatenate([coarse, fine], axis=1).astype(BF16)

    meet(known)

    for _, q in pools:
        send(qp, qg.at[me], qsem.at[0], qsem.at[1], pool=q)
    qg[me] = qp[...]

    wide[...] = jnp.zeros((128, 640), F32)
    wide[0:4, 0:576] = new_in[...].astype(F32)
    for t in range(5):
        n = 64 if t == 4 else 128
        kv[pages, t * 128 : t * 128 + n, :] = wide[:, t * 128 : (t + 1) * 128].T[0:n, :].astype(BF16)
    mb[pages * 16 + 64 :, :] = jnp.full(((rows - pages - 4) * 16, 128), NEG, F32)
    db[pages * 16 + 64 :, :] = jnp.zeros(((rows - pages - 4) * 16, 128), F32)
    for t in range(4):
        nb[t, pages * 16 + 64 :, :] = jnp.zeros(((rows - pages - 4) * 16, 128), F32)

    settle(qg.at[pl.ds(0, 15)], qsem.at[0], qsem.at[1])
    for _, q in pools:
        send(gates_own, gates.at[me], gsem.at[0], gsem.at[1], pool=q)
    gates[me] = gates_own[...]
    wl[0].wait()

    @pl.loop(0, 64, unroll=4)
    def _(j):
        v = qg[j // 4, j % 4].astype(F32)
        qf[pl.ds(pl.multiple_of(j * 16, 16), 16), :] = v[0:16]
        qr[pl.ds(pl.multiple_of(j * 8, 8), 8), :] = v[16:24]

    hot = jnp.where(lane == owner, 1.0, 0.0)
    pick = hot[:, 0:64].astype(BF16)
    for h in range(16):
        s = pl.ds(h, 64, stride=16)
        a = dot(dot(pick, qf[s, :].astype(BF16)).astype(BF16), wuk[h]) * scale
        for t in range(4):
            fq[t, s, :] = a[:, t * 128 : (t + 1) * 128]
        b = dot(pick, qr[pl.ds(h % 8, 64, stride=8), :].astype(BF16)) * scale
        if h >= 8:
            b = jnp.concatenate([b[:, 64:128], b[:, 0:64]], axis=1)
        fq[4, s, :] = b
    more()
    group = lax.broadcasted_iota(jnp.int32, (32, 256), 0) // 16
    spot = lax.broadcasted_iota(jnp.int32, (32, 256), 1) - group * 128

    def pair(i, one, two, lo, hi):
        s = pl.ds(pl.multiple_of(i * 16, 32), 32)
        qa = jnp.concatenate([fq[t, s, :] for t in range(4)], axis=1).astype(BF16)
        qb = fq[4, s, :][:, 0:64].astype(BF16)
        kk = jnp.concatenate([kv[one], kv[two]], axis=1)
        v = dot(qa, kk[0:512, :]) + dot(qb, kk[512:576, :])
        ok = (spot >= lo) & (spot < hi)
        v = jnp.where(ok, v, NEG)
        m = jnp.max(v, axis=1, keepdims=True)
        w = jnp.where(ok, jnp.exp(v - m), 0.0).astype(BF16)
        den = jnp.sum(w.astype(F32), axis=1, keepdims=True)
        num = dot_nt(w, kk[0:512, :])
        mb[s, :] = jnp.broadcast_to(m, (32, 128))
        db[s, :] = jnp.broadcast_to(den, (32, 128))
        for t in range(4):
            nb[t, s, :] = num[:, t * 128 : (t + 1) * 128]

    for k in (0, 2):
        pair(pages + k, pages, pages, group + k, group + k + 1)
    kl.wait()

    @pl.loop(0, pages // 24)
    def _(g):
        for u in range(0, 24, 2):
            i = g * 24 + u
            hi = [jnp.broadcast_to(meta_v[pl.ds(i + n, 1), :], (16, 128)) for n in range(2)]
            hi = jnp.concatenate(hi, axis=0)
            pair(i, i, i + 1, 0, jnp.concatenate([hi, hi], axis=1))


    m = jnp.full((rows, 128), NEG, F32)
    d = jnp.zeros((rows, 128), F32)
    for h in range(16):
        s = pl.ds(h, rows, stride=16)
        m = jnp.where(lane == h, mb[s, :], m)
        d = jnp.where(lane == h, db[s, :], d)
    sf[...] = m
    meta_v[...] = owner
    lp = jnp.full((rows, 128), NEG, F32)
    lr = lp
    for i in range(pages + 4):
        o = meta_v[i : i + 1, :]
        row = sf[i : i + 1, :]
        lp = jnp.maximum(lp, jnp.where(owner == o, row, NEG))
        lr = jnp.maximum(lr, jnp.where(sub == o, row, NEG))
    e = jnp.exp(m - lp)
    hot = hot.T[0:64, :]
    rd = lax.dot_general(
        hot, e * d, (((1,), (0,)), ((), ())), preferred_element_type=F32, precision=lax.Precision.HIGHEST
    )
    wl[1].wait()
    for h in range(16):
        s = pl.ds(h, rows, stride=16)
        a = jnp.concatenate([nb[t, s, :] for t in range(4)], axis=1).astype(BF16)
        vb[:, h * 128 : (h + 1) * 128] = (dot(a, wuv[h]) * e[:, h : h + 1]).astype(BF16)
    full = rd > 0.0
    safe = jnp.where(full, rd, 1.0)
    inv = 1.0 / safe
    sf[...] = jnp.where(full, lr + jnp.log(safe), NEG)
    hot = hot.astype(BF16)
    for h in range(0, 16, 4):
        v = dot(hot, vb[:, h * 128 : (h + 4) * 128])
        for u in range(4):
            of[:, (h + u) * 128 : (h + u + 1) * 128] = v[:, u * 128 : (u + 1) * 128] * inv[:, h + u : h + u + 1]
    for k in range(16):
        pbuf[k] = of[k * 4 : (k + 1) * 4, :].astype(BF16)
        stbuf[k] = sf[k * 4 : (k + 1) * 4, :]
    for _, q in pools:
        send(stbuf.at[q], rst.at[me], ssem.at[0], ssem.at[1], pool=q)
        send(pbuf.at[q], rp.at[me], psem.at[0], psem.at[1], pool=q)
    rst[me] = stbuf[me]
    rp[me] = pbuf[me]
    settle(rst.at[pl.ds(0, 15)], ssem.at[0], ssem.at[1])
    top = rst[0]
    for s in range(1, 16):
        top = jnp.maximum(top, rst[s])
    tot = jnp.zeros((4, 128), F32)
    for s in range(16):
        e = jnp.exp(rst[s] - top)
        rst[s] = e
        tot = tot + e
    inv = 1.0 / tot
    shares = [rst[s] * inv for s in range(16)]
    settle(rp.at[pl.ds(0, 15)], psem.at[0], psem.at[1])

    for h in range(16):
        cols = slice(h * 128, (h + 1) * 128)
        v = jnp.zeros((4, 128), F32)
        for s in range(16):
            v = v + shares[s][:, h : h + 1] * rp[s, :, cols].astype(F32)
        heads[:, cols] = v

    for g in range(8):
        hs[g] = heads[:, g * 256 : (g + 1) * 256].astype(BF16)
    for _, q in reps:
        send(hs.at[q], hb.at[rp_me], hsem.at[0], hsem.at[1], rep=q)
    hb[rp_me] = hs[rp_me]
    wl[2].wait()
    settle(hb.at[pl.ds(0, 7)], hsem.at[0], hsem.at[1])
    for g in range(8):
        hbf[g * 4 : (g + 1) * 4, :] = hb[g].astype(F32)
    pf[...] = dot(hbf[...].astype(BF16), oproj[...])
    for g in range(8):
        ps[g] = pf[g * 4 : (g + 1) * 4, :].astype(BF16)
    for _, q in reps:
        send(ps.at[q], pr.at[rp_me], osem.at[0], osem.at[1], rep=q)
    pr[rp_me] = ps[rp_me]
    settle(pr.at[pl.ds(0, 7)], osem.at[0], osem.at[1])
    proj = pr[0].astype(F32)
    for g in range(1, 8):
        proj = proj + pr[g].astype(F32)
    proj_out[...] = proj
    wl[9].wait()
    wl[10].wait()
    res = hid[...].astype(F32) + proj
    ms = jnp.mean(res * res, axis=1, keepdims=True)
    normed = (res * lax.rsqrt(ms + EPS) * gain[...]).astype(BF16)

    nown[...] = normed
    cp = send(nown, npart, nsem.at[0], nsem.at[1], rep=mate)
    settle(gates.at[pl.ds(0, 15)], gsem.at[0], gsem.at[1])
    cp.wait()
    mine = normed.astype(F32)
    theirs = npart[...].astype(F32)
    blk[0:4, :] = jnp.where(c == 0, mine, theirs)
    blk[4:8, :] = jnp.where(c == 0, theirs, mine)
    for t in range(3):
        s = pl.ds(pl.multiple_of(c * 1024 + STARTS[t], 128), WIDTHS[t])
        xs[t][c, x, z, y] = blk[:, s].astype(BF16)

    whole = pl.ds(0, 4)

    def idx(at):
        return tuple(at[a] if not isinstance(at[a], jax.Array) else pl.ds(at[a], 1) for a in "xzy")

    def near(a, d):
        return (coord[a] + d) % 4

    def share(t, at):
        ref = xs[t].at[(c,) + idx(at)]
        send(ref, ref, fsem.at[0, t], fsem.at[1, t], rep=mate)

    for da in STEPS:
        for db in STEPS:
            if da or db:
                for t in range(3):
                    a, b, _ = ORDERS[t]
                    ref = xs[t].at[(c,) + idx(coord)]
                    send(ref, ref, asem.at[t, 4], asem.at[t, da], **peer(**{a: da, b: db}))
    gm = gates[...].reshape(512, 128)
    for lo, hi in ((0, 256), (256, 512), (512, 704)):
        ids = lax.broadcasted_iota(jnp.int32, (128, hi - lo), 0) % 64
        unit = lax.broadcasted_iota(jnp.int32, (128, hi - lo), 1) + lo
        gws[:, lo:hi] = dot(gm, jnp.where(ids == me * 4 + unit // 176, 1.0, 0.0).astype(BF16))
    for da in STEPS:
        for t in range(3):
            a, b, w = ORDERS[t]
            some = pl.ds(0, 4 if da else 3)
            settle(xs[t].at[(c,) + idx({a: near(a, -da), b: some, w: coord[w]})], asem.at[t, da])
            ref = xs[t].at[(c,) + idx({a: near(a, -da), b: whole, w: coord[w]})]
            for d in range(1, 4):
                send(ref, ref, bsem.at[t, 0], bsem.at[t, d], **peer(**{w: d}))
    for t in range(3):
        a, b, w = ORDERS[t]
        share(t, {a: whole, b: whole, w: coord[w]})
    for d in (1, 3, 2):
        for t in range(3):
            a, b, w = ORDERS[t]
            at = {a: whole, b: whole, w: near(w, -d)}
            settle(xs[t].at[(c,) + idx(at)], bsem.at[t, d])
            share(t, at)
    for t in range(3):
        a, b, w = ORDERS[t]
        settle(rbs[t].at[pl.ds(0, 15)], asem.at[t, 4])
        settle(xs[t].at[(c,) + idx({a: whole, b: whole, w: pl.ds(0, 3)})], bsem.at[t, 0])
        settle(xs[t].at[c], fsem.at[0, t], fsem.at[1, t])

    for t in range(3):
        for h in range(2):
            s = h * 1024 + STARTS[t]
            v = xs[t][h].astype(F32).reshape(512, WIDTHS[t]).astype(BF16)
            xm[:, s : s + WIDTHS[t]] = v

    for i in range(3, 9):
        wl[i].wait()

    col = xm[pl.ds(pl.multiple_of(me * 32, 32), 32), :]
    ga = dot_nt(col, sg[...])
    ua = dot_nt(col, su[...])
    shin[...] = (ga / (1.0 + jnp.exp(-ga)) * ua).astype(BF16)

    for lo, hi in ((0, 256), (256, 512), (512, 704)):
        ga = dot_nt(xm[...], wg[lo:hi, :])
        ua = dot_nt(xm[...], wu[lo:hi, :])
        inner[:, lo:hi] = (ga / (1.0 + jnp.exp(-ga)) * ua * gws[:, lo:hi]).astype(BF16)

    ys = (y0, y1, y2)
    css = (cs0, cs1, cs2)
    crs = (cr0, cr1, cr2)
    cc = []

    def down(t, half):
        wdt = WIDTHS[t]
        cols = pl.ds(pl.multiple_of(half * 1024 + STARTS[t], 128), wdt)
        v = dot(inner[...], wd[:, cols])
        sh = dot(shin[...], sd[:, cols])
        ys[t][...] = v.reshape(4, 4, 4, 8, wdt)
        ys[t][x, z] = ys[t][x, z] + sh.reshape(4, 8, wdt)

    for t in range(3):
        down(t, 1 - c)
        css[t][...] = ys[t][...].astype(BF16)
        cc.append(send(css[t], crs[t], csem.at[0, t], csem.at[1, t], rep=mate))

    sbs = (sb0, sb1, sb2)

    back = (2, 1, 3, 0)
    for t in range(3):
        down(t, c)
        cc[t].wait()
        tot = ys[t][...] + crs[t][...].astype(F32)
        ys[t][...] = tot
        sbs[t][...] = tot.astype(BF16)
        a, b, w = ORDERS[t]
        for da in back:
            for d in range(1, 4):
                src = sbs[t].at[idx({a: near(a, da), b: whole, w: near(w, d)})]
                dst = ras[t].at[(d,) + idx({a: near(a, da), b: whole, w: coord[w] * 0})]
                send(src, dst, dsem.at[t, 4], dsem.at[t, da], **peer(**{w: d}))
    for da in back:
        for t in range(3):
            a, b, w = ORDERS[t]
            at = idx({a: near(a, da), b: whole, w: coord[w] * 0})
            settle(ras[t].at[(pl.ds(1, 3),) + at], dsem.at[t, da])
            v = ys[t][idx({a: near(a, da), b: whole, w: coord[w]})]
            for d in range(1, 4):
                v = v + ras[t][(d,) + at].astype(F32)
            ras[t][(0,) + at] = v.astype(BF16)
            for db in back:
                k = da * 4 + db
                if k:
                    ref = ras[t].at[(0,) + idx({a: near(a, da), b: near(b, db), w: coord[w] * 0})]
                    dst = rbs[t].at[(k,) + (pl.ds(0, 1),) * 3]
                    send(ref, dst, esem.at[0, t], esem.at[1, t], **peer(**{a: da, b: db}))
    for t in range(3):
        a, b, w = ORDERS[t]
        v = ras[t][(0,) + idx({a: coord[a], b: coord[b], w: coord[w] * 0})].astype(F32)
        settle(rbs[t].at[pl.ds(1, 15)], esem.at[0, t], esem.at[1, t])
        settle(ras[t].at[pl.ds(1, 3)], dsem.at[t, 4])
        for k in range(1, 16):
            v = v + rbs[t][k].astype(F32)
        blk[:, STARTS[t] : STARTS[t] + WIDTHS[t]] = v.reshape(8, WIDTHS[t])
    lo, hi = blk[0:4, 0:1024], blk[4:8, 0:1024]
    fs[...] = jnp.where(c == 0, hi, lo).astype(BF16)
    cp = send(fs, fr, lsem.at[0], lsem.at[1], rep=mate)
    own = jnp.where(c == 0, lo, hi)
    cp.wait()
    other = fr[...].astype(F32)
    moe_out[:, 0:1024] = jnp.where(c == 0, own, other)
    moe_out[:, 1024:2048] = jnp.where(c == 0, other, own)


def dma(*shape):
    return pltpu.SemaphoreType.DMA(shape)


def scratch():
    v = pltpu.VMEM
    i32 = jnp.int32
    big = [v((704, 2048), BF16)] * 3 + [v((352, 2048), BF16)] * 3
    out = [v((16, 128, 512), BF16), v((16, 512, 128), BF16), v((49, 576, 128), BF16), v((256, 2048), BF16)]
    out += big + [v((4, 2048), BF16), v((1, 2048), F32), dma(11), pltpu.SemaphoreType.DMA]
    out += [
        v((4, 24, 128), BF16), v((16, 4, 24, 128), BF16), v((1024, 128), F32), v((512, 128), F32),
        v((5, 1024, 128), F32), v((4, 1024, 128), F32), v((1024, 128), F32), v((1024, 128), F32),
        v((64, 128), i32), v((64, 128), i32), v((128, 640), F32),
        v((64, 2048), BF16), v((64, 2048), F32), v((64, 128), F32), v((16, 4, 2048), BF16),
        v((16, 4, 128), F32), dma(2),
    ]
    out += [
        v((16, 4, 2048), BF16), v((16, 4, 128), F32), v((32, 128), BF16), v((16, 32, 128), BF16), v((4, 2048), F32),
        v((8, 4, 256), BF16), v((8, 4, 256), BF16), v((32, 256), F32), v((32, 2048), F32),
        v((8, 4, 2048), BF16), v((8, 4, 2048), BF16), v((4, 2048), BF16), v((4, 2048), BF16),
        v((8, 2048), F32),
    ]
    out += [v((2, 4, 4, 4, 8, w), BF16) for w in WIDTHS]
    out += [v((512, 2048), BF16), v((512, 704), F32), v((512, 704), BF16), v((32, 352), BF16)]
    out += [v((4, 4, 4, 8, w), F32) for w in WIDTHS]
    out += [v((4, 4, 4, 8, w), BF16) for w in WIDTHS] * 3

    def shape(t):
        return tuple(1 if a == ORDERS[t][2] else 4 for a in "xzy") + (8, WIDTHS[t])

    out += [v((4,) + shape(t), BF16) for t in range(3)]
    out += [v((16, 1, 1, 1, 8, w), BF16) for w in WIDTHS]
    out += [v((4, 1024), BF16), v((4, 1024), BF16)]
    out += [
        dma(2), dma(2), dma(2), dma(2), dma(2), dma(2),
        dma(3, 5), dma(3, 4), dma(2, 3), dma(2, 3), dma(3, 5), dma(2, 3), dma(2),
    ]
    return out


def params(cid):
    return pltpu.CompilerParams(vmem_limit_bytes=LIMIT, collective_id=cid, has_side_effects=True)


def call(q, table, lens, new, routes, gates, *rest):
    sds = jax.ShapeDtypeStruct
    return pl.pallas_call(
        layer,
        out_shape=(sds((4, 2048), F32), sds((4, 2048), F32)),
        in_specs=[VM] * 6 + [HBM] * 12,
        out_specs=(VM, VM),
        scratch_shapes=scratch(),
        compiler_params=params(0),
        name="layer",
    )(q, table, lens, new, routes, gates, *rest)


def shards(
    hidden,
    queries,
    new_kv,
    kv_cache,
    block_table,
    seq_lens,
    w_uk,
    w_uv,
    o_proj,
    norm_gain,
    routes,
    gate_weights,
    w_gate,
    w_up,
    w_down,
    shared_gate,
    shared_up,
    shared_down,
):
    wide = lambda w: jnp.swapaxes(w, -1, -2)
    flat = lambda w: w.reshape(-1, w.shape[-1])
    proj, moe = call(
        queries[0], block_table[0], seq_lens, new_kv[0],
        routes[0].T, gate_weights[0].T, hidden[0], norm_gain[None],
        w_uk, w_uv, wide(kv_cache[0]), o_proj, flat(wide(w_gate)), flat(wide(w_up)), flat(w_down),
        wide(shared_gate), wide(shared_up), shared_down,
    )
    layer_out = (hidden[0].astype(F32) + proj + moe).astype(BF16)
    return proj.astype(BF16)[None], layer_out[None]


def solution(mesh):
    placed = (
        P("rep", "pool", None),
        P("rep", "pool", None, None),
        P("rep", "pool", None),
        P("rep", "pool", None, None),
        P("rep", None, None),
        P("rep", None),
        P(),
        P(),
        P("rep", None),
        P(),
        P("pool", None, None, None),
        P("pool", None, None, None),
        P("pool", None, "rep"),
        P("pool", None, "rep"),
        P("pool", "rep", None),
        P(None, "rep"),
        P(None, "rep"),
        P("rep", None),
    )
    return jax.shard_map(
        shards,
        mesh=mesh,
        in_specs=placed,
        out_specs=(P("rep", "pool", None), P("rep", "pool", None)),
        check_vma=False,
    )
```
